256 devices in a mesh: head: 8 (over z), tok: 32 (over x, y, core).
Axes of the slice: x: 4, y: 4, z: 8, core: 2. Of those that a mesh axis runs over, the one named last changes fastest.
Arguments:
- teacher_q: bfloat16 [4096, 2048], P('tok', 'head'), may hold values from -48 to 48
- student_q: bfloat16 [4096, 2048], P('tok', 'head'), may hold values from -48 to 48
- owner_table: int32 [32, 32], replicated, may hold values from -1 to 31, as said below
Outputs:
- student_grad: bfloat16 [4096, 2048], P('tok', 'head')
- divergence: float32 [32], P('head')
The draws below stay inside these ranges and needn't reach their ends.
Inputs may be any that keep to these rules, and one draw needn't show every extreme that they name: `owner_table`: Symmetric; every diagonal entry is an owner; an owner is a tok index; each tok index owns at most 8 pairs i <= j, and some tok index owns exactly 8 in every draw.
All inputs are finite; a program needn't handle non-finite values.
Results may differ from the reference program's by a relative error of at most 0.0049.
Values may be sent and summed in bfloat16 or wider, within the bound.
No kernel may reach another device: no remote copies, remote signals or barrier semaphores. Data moves between devices by JAX's collectives and lax.ppermute only.
A program may use at most 64 MiB of HBM per device.

```python
import jax
import jax.numpy as jnp
import numpy as np
from jax import lax

HEAD_DIM = 64
TOK_DEV = 128
REL_HEADS = 32
TOKENS = 4096
BLOCKS = 32
PAIR_MOST = 8


def draw_queries(key):
    base = jnp.clip(jax.random.normal(key, (TOKENS, REL_HEADS, HEAD_DIM)), -6.0, 6.0)
    return base.reshape(TOKENS, REL_HEADS * HEAD_DIM).astype(jnp.bfloat16)


def draw_teacher_q(key, part):
    return draw_queries(jax.random.fold_in(key, 11))


def draw_student_q(key, part):
    return draw_queries(jax.random.fold_in(key, 23))


def draw_owner_table(key, part):
    upper_rows, upper_cols = np.triu_indices(BLOCKS)
    every_place = np.arange(upper_rows.shape[0])
    diagonal_places = every_place[upper_rows == upper_cols]
    other_places = every_place[upper_rows != upper_cols]
    key_diag, key_other, key_caps, key_owner = jax.random.split(jax.random.fold_in(key, 7), 4)
    ordering = jnp.concatenate([jax.random.permutation(key_diag, jnp.asarray(diagonal_places, jnp.int32)), jax.random.permutation(key_other, jnp.asarray(other_places, jnp.int32))])
    capacity = jax.random.randint(key_caps, (BLOCKS,), 1, PAIR_MOST + 1).astype(jnp.int32).at[0].set(PAIR_MOST)
    owners_order = jax.random.permutation(key_owner, BLOCKS).astype(jnp.int32)
    bounds = jnp.cumsum(capacity)
    positions = jnp.arange(upper_rows.shape[0], dtype=jnp.int32)
    which = jnp.sum((bounds[None, :] <= positions[:, None]).astype(jnp.int32), axis=1)
    owners = jnp.where(which < BLOCKS, owners_order[jnp.minimum(which, BLOCKS - 1)], -1)
    pair_rows = jnp.asarray(upper_rows, jnp.int32)[ordering]
    pair_cols = jnp.asarray(upper_cols, jnp.int32)[ordering]
    table = jnp.full((BLOCKS, BLOCKS), -1, jnp.int32)
    table = table.at[pair_rows, pair_cols].set(owners)
    return table.at[pair_cols, pair_rows].set(owners)


def setup_inputs(seed: int = 0) -> dict:
    splits = jax.random.split(jax.random.key(seed), 4)
    teacher_q = draw_teacher_q(jax.random.fold_in(splits[3], 71), 0)
    student_q = draw_student_q(jax.random.fold_in(splits[3], 71), 0)
    owner_table = draw_owner_table(jax.random.fold_in(splits[3], 71), 0)
    return {"teacher_q": teacher_q, "student_q": student_q, "owner_table": owner_table}


floor_value = -1e+30
distill_weight = 32.0

def reference(teacher_q, student_q, owner_table):
    scale = HEAD_DIM ** (-0.5)
    length = teacher_q.shape[0]
    inside = jnp.repeat(jnp.repeat(owner_table >= 0, TOK_DEV, axis=0), TOK_DEV, axis=1)
    heads_teacher = teacher_q.reshape(length, REL_HEADS, HEAD_DIM).transpose(1, 0, 2)
    heads_student = student_q.reshape(length, REL_HEADS, HEAD_DIM).transpose(1, 0, 2)

    def logsum(scores):
        masked = jnp.where(inside, scores, floor_value)
        highest = jnp.max(masked, axis=1)
        return highest + jnp.log(jnp.sum(jnp.exp(masked - highest[:, None]), axis=1))

    def one_head(queries):
        teacher_head, student_head = queries
        teacher_scores = jnp.dot(teacher_head.astype(jnp.float32), teacher_head.T.astype(jnp.float32), preferred_element_type=jnp.float32) * scale
        student_scores = jnp.dot(student_head.astype(jnp.float32), student_head.T.astype(jnp.float32), preferred_element_type=jnp.float32) * scale
        teacher_logsum = logsum(teacher_scores)
        student_logsum = logsum(student_scores)
        teacher_prob = jnp.where(inside, jnp.exp(teacher_scores - teacher_logsum[:, None]), 0.0)
        student_prob = jnp.where(inside, jnp.exp(student_scores - student_logsum[:, None]), 0.0)
        row_div = jnp.sum(teacher_prob * (teacher_scores - student_scores), axis=1) - teacher_logsum + student_logsum
        score_gap = student_prob - teacher_prob
        symmetric = (score_gap + score_gap.T).astype(jnp.bfloat16)
        gradient = jnp.dot(symmetric.astype(jnp.float32), student_head.astype(jnp.float32), preferred_element_type=jnp.float32) * (scale * distill_weight)
        return (gradient.astype(jnp.bfloat16), jnp.mean(row_div))
    gradients, divergence = lax.map(one_head, (heads_teacher, heads_student))
    return (gradients.transpose(1, 0, 2).reshape(length, REL_HEADS * HEAD_DIM), divergence)
```

```python
import jax
import jax.numpy as jnp
from jax import lax
from jax.experimental import pallas as pl
from jax.experimental.pallas import tpu as pltpu
from jax.sharding import PartitionSpec as P

HEAD = 64
ROWS = 128
BLOCKS = 32
LINE = 4
LOG2E = 1.4426950408889634
LN2 = 0.6931471805599453
SCALE = HEAD**-0.5
WEIGHT = 32.0 * SCALE
SUM_LIMIT = 2.0**100
FLOOR = -1e30
UNROLL = 4
LIST_AT = 8
OWN_AT = LIST_AT + BLOCKS * BLOCKS + 8
PLAN_LEN = OWN_AT + LINE * BLOCKS + 8
VMEM = pl.BlockSpec(memory_space=pltpu.VMEM)
SMEM = pl.BlockSpec(memory_space=pltpu.SMEM)


def my_index():
    return lax.axis_index("tok")


def exchanged(array, bits):
    return lax.ppermute(array, "tok", [(i, i ^ bits) for i in range(BLOCKS)])


def slice_kernel(teacher_ref, student_ref, *out_refs):
    x = my_index() >> 3
    for head in range(LINE):
        at = slice(head * HEAD, head * HEAD + HEAD)
        both = jnp.concatenate([teacher_ref[:, at], student_ref[:, at]], axis=1)
        for turn, out_ref in enumerate(out_refs):

            @pl.when(x == (head ^ turn))
            def _():
                out_ref[...] = both


def plan_kernel(table_ref, plan_ref):
    me = my_index()

    def listed(row, first, prefix):
        at = first
        for column in range(BLOCKS):
            plan_ref[at] = prefix + column
            at = at + (table_ref[row, column] >= 0).astype(jnp.int32)
        return at

    end = lax.fori_loop(0, BLOCKS, lambda i, at: listed(i, at, i * BLOCKS), jnp.int32(LIST_AT))
    for k in range(UNROLL):
        plan_ref[end + k] = BLOCKS * BLOCKS
    plan_ref[0] = end - LIST_AT
    end = lax.fori_loop(
        0, LINE, lambda b, at: listed(me ^ (b << 3), at, b * BLOCKS), jnp.int32(OWN_AT)
    )
    for k in range(UNROLL):
        plan_ref[end + k] = LINE * BLOCKS
    plan_ref[1] = end - OWN_AT


def main_kernel(
    plan_ref,
    half_ref,
    other_ref,
    *refs,
):
    out_refs = refs[:LINE]
    rows_ref, wide_ref, acc_ref, top_ref, inv_ref, grad_ref, col_ref = refs[LINE:]
    me = my_index()

    for slot in range(BLOCKS):
        code = ((slot & 3) << 3) | (((slot >> 2) & 3) << 1) | (slot >> 4)
        block = me ^ code
        tile = half_ref[slot] if slot < 16 else other_ref[slot - 16]
        rows_ref[block] = tile
        flipped = tile.astype(jnp.float32).T.astype(jnp.bfloat16)
        zero = jnp.zeros((HEAD, ROWS), jnp.bfloat16)
        wide_ref[block, :, :ROWS] = jnp.concatenate([flipped[:HEAD], zero], axis=0)
        wide_ref[block, :, ROWS:] = jnp.concatenate([zero, flipped[HEAD:]], axis=0)
    wide_ref[BLOCKS] = jnp.zeros((ROWS, 2 * ROWS), jnp.bfloat16)
    pairs = plan_ref[0]
    own_pairs = plan_ref[1]

    def scores(left, right):
        return jnp.dot(rows_ref[left], wide_ref[right], preferred_element_type=jnp.float32)

    def folded(a):
        return jnp.sum(a.reshape(ROWS // 8, 8, ROWS), axis=0)

    def totals(exps, raw):
        teacher, student = exps[:, :ROWS], exps[:, ROWS:]
        gap = teacher * (raw[:, :ROWS] - raw[:, ROWS:])
        return folded(teacher), folded(student), folded(gap)

    def added(row, parts):
        for k, part in enumerate(parts):
            acc_ref[row, k] += part

    acc_ref[...] = jnp.zeros_like(acc_ref)

    def sum_turn(group, carry):
        done = []
        for k in range(UNROLL):
            word = plan_ref[LIST_AT + group * UNROLL + k]
            row, column = word >> 5, word & (BLOCKS - 1)
            raw = scores(column, row)
            done.append((row, totals(jnp.exp2(raw * (SCALE * LOG2E)), raw)))
        for row, parts in done:
            added(row, parts)
        return carry

    lax.fori_loop(0, (pairs + UNROLL - 1) // UNROLL, sum_turn, 0)

    def row_sums(k):
        return jnp.sum(acc_ref[:BLOCKS, k], axis=1)

    teacher_sum, student_sum, gap_sum = row_sums(0), row_sums(1), row_sums(2)
    fine = (
        (teacher_sum < SUM_LIMIT) & (student_sum < SUM_LIMIT) & (jnp.abs(gap_sum) < SUM_LIMIT)
    )
    safe = jnp.min(fine.astype(jnp.float32)) > 0.5
    grad_ref[...] = jnp.zeros_like(grad_ref)

    def finished(mean_div):
        high = mean_div.astype(jnp.bfloat16).astype(jnp.float32)
        middle = (mean_div - high).astype(jnp.bfloat16).astype(jnp.float32)
        low = mean_div - high - middle
        lane = lax.broadcasted_iota(jnp.int32, (ROWS, ROWS), 1)
        tail = jnp.where(lane == HEAD, high, jnp.where(lane == HEAD + 1, middle, low))
        for b, out_ref in enumerate(out_refs):
            moved = pltpu.roll(grad_ref[b] * WEIGHT, HEAD, 1)
            out_ref[...] = jnp.where(lane < HEAD, moved, tail).astype(jnp.bfloat16)

    def along_rows(row):
        return jnp.broadcast_to(row, (ROWS, ROWS)).T

    def mean_of(per_row):
        return jnp.sum(per_row, keepdims=True).reshape(1, 1) * (1.0 / (BLOCKS * ROWS))

    def gradient(word, weigh):
        b, column = word >> 5, word & (BLOCKS - 1)
        raw = scores(me ^ ((b & 3) << 3), column)
        symmetric = weigh(b, column, raw)
        return b, jnp.dot(
            symmetric.astype(jnp.bfloat16), rows_ref[column], preferred_element_type=jnp.float32
        )

    @pl.when(safe)
    def _():
        inv_ref[0] = 1.0 / teacher_sum
        inv_ref[1] = 1.0 / student_sum
        for b in range(LINE):
            for k in range(2):
                col_ref[b, k] = along_rows(inv_ref[k, pl.ds(me ^ (b << 3), 1), :])

        def weigh(b, column, raw):
            exps = jnp.exp2(raw * (SCALE * LOG2E))
            teacher_inv = col_ref[b, 0] + inv_ref[0, pl.ds(column, 1), :]
            student_inv = col_ref[b, 1] + inv_ref[1, pl.ds(column, 1), :]
            return exps[:, ROWS:] * student_inv - exps[:, :ROWS] * teacher_inv

        def grad_turn(group, carry):
            done = [
                gradient(plan_ref[OWN_AT + group * UNROLL + k], weigh) for k in range(UNROLL)
            ]
            for b, part in done:
                grad_ref[b] += part
            return carry

        lax.fori_loop(0, (own_pairs + UNROLL - 1) // UNROLL, grad_turn, 0)
        per_row = (
            gap_sum * inv_ref[0] * SCALE - jnp.log(teacher_sum) + jnp.log(student_sum)
        )
        finished(mean_of(per_row))

    @pl.when(jnp.logical_not(safe))
    def _():
        top_ref[...] = jnp.full_like(top_ref, FLOOR)

        def top_turn(n, carry):
            word = plan_ref[LIST_AT + n]
            row, column = word >> 5, word & (BLOCKS - 1)
            raw = jnp.max(scores(column, row), axis=0, keepdims=True) * SCALE
            top_ref[0, pl.ds(row, 1), :] = jnp.maximum(top_ref[0, pl.ds(row, 1), :], raw[:, :ROWS])
            top_ref[1, pl.ds(row, 1), :] = jnp.maximum(top_ref[1, pl.ds(row, 1), :], raw[:, ROWS:])
            return carry

        lax.fori_loop(0, pairs, top_turn, 0)
        acc_ref[...] = jnp.zeros_like(acc_ref)

        def shifted_turn(n, carry):
            word = plan_ref[LIST_AT + n]
            row, column = word >> 5, word & (BLOCKS - 1)
            raw = scores(column, row)
            top = jnp.concatenate(
                [top_ref[0, pl.ds(row, 1), :], top_ref[1, pl.ds(row, 1), :]], axis=1
            )
            added(row, totals(jnp.exp(raw * SCALE - top), raw))
            return carry

        lax.fori_loop(0, pairs, shifted_turn, 0)
        teacher_sum, student_sum, gap_sum = row_sums(0), row_sums(1), row_sums(2)
        inv_ref[0] = top_ref[0] + jnp.log(teacher_sum)
        inv_ref[1] = top_ref[1] + jnp.log(student_sum)
        for b in range(LINE):
            for k in range(2):
                col_ref[b, k] = along_rows(inv_ref[k, pl.ds(me ^ (b << 3), 1), :])

        def weigh(b, column, raw):
            teacher, student = raw[:, :ROWS] * SCALE, raw[:, ROWS:] * SCALE
            rows_gap = jnp.exp(student - col_ref[b, 1]) - jnp.exp(teacher - col_ref[b, 0])
            cols_gap = jnp.exp(student - inv_ref[1, pl.ds(column, 1), :]) - jnp.exp(
                teacher - inv_ref[0, pl.ds(column, 1), :]
            )
            return rows_gap + cols_gap

        def grad_turn(n, carry):
            b, part = gradient(plan_ref[OWN_AT + n], weigh)
            grad_ref[b] += part
            return carry

        lax.fori_loop(0, own_pairs, grad_turn, 0)
        finished(mean_of(gap_sum / teacher_sum * SCALE - inv_ref[0] + inv_ref[1]))


def assemble_kernel(*refs):
    in_refs, (grad_ref, div_ref) = refs[:LINE], refs[LINE:]
    x = my_index() >> 3
    lane = lax.broadcasted_iota(jnp.int32, (16, ROWS), 1)
    holds_div = (lane >= HEAD) & (lane < HEAD + 3) & (
        lax.broadcasted_iota(jnp.int32, (16, ROWS), 0) == 0
    )
    for case in range(LINE):

        @pl.when(x == case)
        def _():
            for head in range(LINE):
                from_ref = in_refs[head ^ case]
                grad_ref[:, head * HEAD : head * HEAD + HEAD] = from_ref[:, :HEAD]
                parts = jnp.where(holds_div, from_ref[:16].astype(jnp.float32), 0.0)
                div_ref[head] = jnp.sum(parts)


def per_device(teacher_q, student_q, owner_table):
    tile = jax.ShapeDtypeStruct((ROWS, ROWS), jnp.bfloat16)
    slices = pl.pallas_call(
        slice_kernel,
        out_shape=[tile] * LINE,
        in_specs=[VMEM, VMEM],
        out_specs=[VMEM] * LINE,
        name="slice_heads",
    )(teacher_q, student_q)
    plan = pl.pallas_call(
        plan_kernel,
        out_shape=jax.ShapeDtypeStruct((PLAN_LEN,), jnp.int32),
        in_specs=[SMEM],
        out_specs=SMEM,
        name="list_pairs",
    )(owner_table)
    line = jnp.stack([slices[0]] + [exchanged(slices[b], b << 3) for b in (1, 2, 3)])
    half = jnp.concatenate([line] + [exchanged(line, a << 1) for a in (1, 2, 3)])
    other = exchanged(half, 1)
    grads = pl.pallas_call(
        main_kernel,
        out_shape=[tile] * LINE,
        in_specs=[SMEM, VMEM, VMEM],
        out_specs=[VMEM] * LINE,
        scratch_shapes=[
            pltpu.VMEM((BLOCKS, ROWS, ROWS), jnp.bfloat16),
            pltpu.VMEM((BLOCKS + 1, ROWS, 2 * ROWS), jnp.bfloat16),
            pltpu.VMEM((BLOCKS + 1, 3, 8, ROWS), jnp.float32),
            pltpu.VMEM((2, BLOCKS, ROWS), jnp.float32),
            pltpu.VMEM((2, BLOCKS, ROWS), jnp.float32),
            pltpu.VMEM((LINE + 1, ROWS, ROWS), jnp.float32),
            pltpu.VMEM((LINE + 1, 2, ROWS, ROWS), jnp.float32),
        ],
        compiler_params=pltpu.CompilerParams(vmem_limit_bytes=24 << 20),
        name="sums_and_gradient",
    )(plan, half, other)
    back = [grads[0]] + [exchanged(grads[b], b << 3) for b in (1, 2, 3)]
    return pl.pallas_call(
        assemble_kernel,
        out_shape=[
            jax.ShapeDtypeStruct(teacher_q.shape, jnp.bfloat16),
            jax.ShapeDtypeStruct((LINE,), jnp.float32),
        ],
        in_specs=[VMEM] * LINE,
        out_specs=[VMEM, SMEM],
        name="assemble",
    )(*back)


def solution(mesh):
    placed = (P("tok", "head"), P("tok", "head"), P())
    return jax.shard_map(
        lambda *arrays: tuple(per_device(*arrays)),
        mesh=mesh,
        in_specs=placed,
        out_specs=(P("tok", "head"), P("head")),
        check_vma=False,
    )
```

```python
import jax
import jax.numpy as jnp
from jax import lax
from jax.experimental import pallas as pl
from jax.experimental.pallas import tpu as pltpu
from jax.sharding import PartitionSpec as P

HEAD = 64
ROWS = 128
BLOCKS = 32
SIDE = BLOCKS // 2
LINE = 4
LOG2E = 1.4426950408889634
SCALE = HEAD**-0.5
WEIGHT = 32.0 * SCALE
SUM_LIMIT = 2.0**100
FLOOR = -1e30
UNROLL = 16
CHUNK = 4
OWN_UNROLL = 2
NEAR_AT = 8
FAR_AT = NEAR_AT + SIDE * SIDE + UNROLL
OWN_NEAR_AT = FAR_AT + SIDE * SIDE + UNROLL
OWN_FAR_AT = OWN_NEAR_AT + LINE * SIDE + CHUNK * OWN_UNROLL + CHUNK
PLAN_LEN = OWN_FAR_AT + LINE * SIDE + CHUNK * OWN_UNROLL + CHUNK
DIV_AT = 2 * SIDE
FLAG_AT = DIV_AT + 1
SENT = DIV_AT + 8
VMEM = pl.BlockSpec(memory_space=pltpu.VMEM)
SMEM = pl.BlockSpec(memory_space=pltpu.SMEM)


def my_index():
    return lax.axis_index("tok")


def exchanged(array, bits):
    return lax.ppermute(array, "tok", [(i, i ^ bits) for i in range(BLOCKS)])


def slice_kernel(teacher_ref, student_ref, *out_refs):
    x = my_index() >> 3
    for head in range(LINE):
        at = slice(head * HEAD, head * HEAD + HEAD)
        both = jnp.concatenate([teacher_ref[:, at], student_ref[:, at]], axis=1)
        for turn, out_ref in enumerate(out_refs):

            @pl.when(x == (head ^ turn))
            def _():
                out_ref[...] = both


def plan_kernel(table_ref, plan_ref):
    me = my_index()
    core = me & 1

    def listed(row, side, first, prefix):
        at = first
        for k in range(SIDE):
            plan_ref[at] = prefix + k
            at = at + (table_ref[row, 2 * k + side] >= 0).astype(jnp.int32)
        return at

    def filled(at, count, word):
        for k in range(count):
            plan_ref[at + k] = word

    for slot, (first, side) in enumerate(((NEAR_AT, core), (FAR_AT, 1 - core))):
        end = lax.fori_loop(
            0,
            SIDE,
            lambda i, at: listed(2 * i + core, side, at, i * BLOCKS),
            jnp.int32(first),
        )
        filled(end, UNROLL, SIDE * BLOCKS)
        plan_ref[slot] = end - first
    for slot, (first, side) in enumerate(((OWN_NEAR_AT, core), (OWN_FAR_AT, 1 - core))):

        def own(b, at):
            end = listed(me ^ (b << 3), side, at, b * BLOCKS)
            filled(end, CHUNK - 1, b * BLOCKS + SIDE)
            return first + (((end - first + CHUNK - 1) >> 2) << 2)

        end = lax.fori_loop(0, LINE, own, jnp.int32(first))
        filled(end, CHUNK * OWN_UNROLL, LINE * BLOCKS + SIDE)
        plan_ref[2 + slot] = (end - first) >> 2


def spread(in_ref, rows_ref, wide_ref):
    me = my_index()
    zero = jnp.zeros((HEAD, ROWS), jnp.bfloat16)
    for slot in range(SIDE):
        at = (me >> 1) ^ (((slot & 3) << 2) | (slot >> 2))
        tile = in_ref[slot]
        rows_ref[at] = tile
        flipped = tile.astype(jnp.float32).T.astype(jnp.bfloat16)
        wide_ref[at, :, :ROWS] = jnp.concatenate([flipped[:HEAD], zero], axis=0)
        wide_ref[at, :, ROWS:] = jnp.concatenate([zero, flipped[HEAD:]], axis=0)
    rows_ref[SIDE] = jnp.zeros((ROWS, ROWS), jnp.bfloat16)
    wide_ref[SIDE] = jnp.zeros((ROWS, 2 * ROWS), jnp.bfloat16)


def scores(left, right):
    return jnp.dot(left, right, preferred_element_type=jnp.float32)


def folded(a):
    return jnp.sum(a.reshape(ROWS // 8, 8, ROWS), axis=0)


def totals(exps, raw):
    teacher, student = exps[:, :ROWS], exps[:, ROWS:]
    gap = teacher * (raw[:, :ROWS] - raw[:, ROWS:])
    return folded(teacher), folded(student), folded(gap)


def add_totals(plan_ref, first, pairs, rows_ref, wide_ref, acc_ref):
    def turn(group, carry):
        done = []
        for k in range(UNROLL):
            word = plan_ref[first + group * UNROLL + k]
            row, column = word >> 5, word & (BLOCKS - 1)
            raw = scores(rows_ref[column], wide_ref[row])
            done.append((row, totals(jnp.exp2(raw * (SCALE * LOG2E)), raw)))
        for row, parts in done:
            for k, part in enumerate(parts):
                acc_ref[row, k] += part
        return carry

    lax.fori_loop(0, (pairs + UNROLL - 1) // UNROLL, turn, 0)


def near_kernel(plan_ref, half_ref, rows_ref, wide_ref, acc_ref):
    spread(half_ref, rows_ref, wide_ref)
    acc_ref[...] = jnp.zeros_like(acc_ref)
    add_totals(plan_ref, NEAR_AT, plan_ref[0], rows_ref, wide_ref, acc_ref)


def far_kernel(
    plan_ref,
    other_ref,
    near_rows_ref,
    near_wide_ref,
    near_acc_ref,
    rows_ref,
    wide_ref,
    sent_ref,
    acc_ref,
    top_ref,
):
    spread(other_ref, rows_ref, wide_ref)
    acc_ref[...] = near_acc_ref[...]
    add_totals(plan_ref, FAR_AT, plan_ref[1], rows_ref, near_wide_ref, acc_ref)

    def row_sums(k):
        return jnp.sum(acc_ref[:SIDE, k], axis=1)

    def finished(teacher_log, student_log, gap_mean, flag):
        sent_ref[:SIDE] = teacher_log
        sent_ref[SIDE : 2 * SIDE] = student_log
        per_row = gap_mean * SCALE - teacher_log + student_log
        row = lax.broadcasted_iota(jnp.int32, (8, ROWS), 0)
        sent_ref[DIV_AT:] = jnp.where(
            row == 0, jnp.sum(per_row, axis=0, keepdims=True), jnp.where(row == 1, flag, 0.0)
        )

    teacher_sum, student_sum, gap_sum = row_sums(0), row_sums(1), row_sums(2)
    fine = (
        (teacher_sum < SUM_LIMIT) & (student_sum < SUM_LIMIT) & (jnp.abs(gap_sum) < SUM_LIMIT)
    )
    safe = jnp.min(fine.astype(jnp.float32)) > 0.5

    @pl.when(safe)
    def _():
        finished(jnp.log(teacher_sum), jnp.log(student_sum), gap_sum / teacher_sum, 0.0)

    @pl.when(jnp.logical_not(safe))
    def _():
        top_ref[...] = jnp.full_like(top_ref, FLOOR)
        acc_ref[...] = jnp.zeros_like(acc_ref)
        lists = ((NEAR_AT, plan_ref[0], near_rows_ref), (FAR_AT, plan_ref[1], rows_ref))

        def each_pair(act):
            for first, pairs, left_ref in lists:

                def turn(n, carry):
                    word = plan_ref[first + n]
                    row, column = word >> 5, word & (BLOCKS - 1)
                    act(row, scores(left_ref[column], near_wide_ref[row]))
                    return carry

                lax.fori_loop(0, pairs, turn, 0)

        def raise_top(row, raw):
            top = jnp.max(raw, axis=0, keepdims=True) * SCALE
            for k in range(2):
                at = (k, pl.ds(row, 1), slice(None))
                top_ref[at] = jnp.maximum(top_ref[at], top[:, k * ROWS : (k + 1) * ROWS])

        def add_shifted(row, raw):
            top = jnp.concatenate([top_ref[k, pl.ds(row, 1), :] for k in range(2)], axis=1)
            for k, part in enumerate(totals(jnp.exp(raw * SCALE - top), raw)):
                acc_ref[row, k] += part

        each_pair(raise_top)
        each_pair(add_shifted)
        teacher_sum, student_sum, gap_sum = row_sums(0), row_sums(1), row_sums(2)
        finished(
            top_ref[0] + jnp.log(teacher_sum),
            top_ref[1] + jnp.log(student_sum),
            gap_sum / teacher_sum,
            1.0,
        )


def along_rows(row):
    return jnp.broadcast_to(row, (ROWS, ROWS)).T


def own_at(b):
    return (my_index() >> 1) ^ ((b & 3) << 2)


def is_safe(sent_ref):
    return jnp.max(sent_ref[FLAG_AT : FLAG_AT + 1]) < 0.5


def fill_columns(col_ref, value, near_sent_ref):
    for b in range(LINE):
        for k in range(2):
            row = near_sent_ref[pl.ds(own_at(b) + k * SIDE, 1), :]
            col_ref[b, k] = along_rows(value(row))


def safe_gradient(plan_ref, first, chunks, near_rows_ref, rows_ref, wide_ref, sent_ref, inv_ref, col_ref, grad_ref):
    inv_ref[...] = jnp.zeros_like(inv_ref)
    for k in range(2):
        inv_ref[k, :SIDE] = jnp.exp(-sent_ref[k * SIDE : (k + 1) * SIDE])

    def chunk_part(at):
        words = [plan_ref[at + k] for k in range(CHUNK)]
        b = words[0] >> 5
        columns = [w & (BLOCKS - 1) for w in words]
        wide = jnp.concatenate([wide_ref[c] for c in columns], axis=1)
        exps = jnp.exp2(scores(near_rows_ref[own_at(b)], wide) * (SCALE * LOG2E))
        symmetric = []
        for k, c in enumerate(columns):
            at_k = 2 * ROWS * k
            teacher, student = exps[:, at_k : at_k + ROWS], exps[:, at_k + ROWS : at_k + 2 * ROWS]
            teacher_inv = col_ref[b, 0] + inv_ref[0, pl.ds(c, 1), :]
            student_inv = col_ref[b, 1] + inv_ref[1, pl.ds(c, 1), :]
            symmetric.append((student * student_inv - teacher * teacher_inv).astype(jnp.bfloat16))
        right = jnp.concatenate([rows_ref[c] for c in columns], axis=0)
        return b, scores(jnp.concatenate(symmetric, axis=1), right)

    def turn(group, carry):
        done = [
            chunk_part(first + (group * OWN_UNROLL + k) * CHUNK) for k in range(OWN_UNROLL)
        ]
        for b, part in done:
            grad_ref[b] += part
        return carry

    lax.fori_loop(0, (chunks + OWN_UNROLL - 1) // OWN_UNROLL, turn, 0)


def shifted_gradient(plan_ref, first, chunks, near_rows_ref, rows_ref, wide_ref, sent_ref, inv_ref, col_ref, grad_ref):
    inv_ref[...] = jnp.zeros_like(inv_ref)
    for k in range(2):
        inv_ref[k, :SIDE] = sent_ref[k * SIDE : (k + 1) * SIDE]

    def turn(n, carry):
        word = plan_ref[first + n]
        b, c = word >> 5, word & (BLOCKS - 1)

        @pl.when(c < SIDE)
        def _():
            raw = scores(near_rows_ref[own_at(b)], wide_ref[c]) * SCALE
            teacher, student = raw[:, :ROWS], raw[:, ROWS:]
            row_gap = jnp.exp(student - col_ref[b, 1]) - jnp.exp(teacher - col_ref[b, 0])
            column_gap = jnp.exp(student - inv_ref[1, pl.ds(c, 1), :]) - jnp.exp(
                teacher - inv_ref[0, pl.ds(c, 1), :]
            )
            grad_ref[b] += scores((row_gap + column_gap).astype(jnp.bfloat16), rows_ref[c])

        return carry

    lax.fori_loop(0, chunks * CHUNK, turn, 0)


def near_grad_kernel(plan_ref, rows_ref, wide_ref, sent_ref, grad_ref, col_ref, inv_ref):
    grad_ref[...] = jnp.zeros_like(grad_ref)
    col_ref[LINE] = jnp.zeros((2, ROWS, ROWS), jnp.float32)
    rest = (plan_ref, OWN_NEAR_AT, plan_ref[2], rows_ref, rows_ref, wide_ref, sent_ref)
    safe = is_safe(sent_ref)

    @pl.when(safe)
    def _():
        fill_columns(col_ref, lambda row: jnp.exp(-row), sent_ref)
        safe_gradient(*rest, inv_ref, col_ref, grad_ref)

    @pl.when(jnp.logical_not(safe))
    def _():
        fill_columns(col_ref, lambda row: row, sent_ref)
        shifted_gradient(*rest, inv_ref, col_ref, grad_ref)


def far_grad_kernel(
    plan_ref,
    near_rows_ref,
    rows_ref,
    wide_ref,
    near_sent_ref,
    sent_ref,
    near_grad_ref,
    near_col_ref,
    *refs,
):
    out_refs, (inv_ref, grad_ref, col_ref) = refs[:LINE], refs[LINE:]
    grad_ref[...] = near_grad_ref[...]
    rest = (plan_ref, OWN_FAR_AT, plan_ref[3], near_rows_ref, rows_ref, wide_ref, sent_ref)
    safe = is_safe(sent_ref) & is_safe(near_sent_ref)

    @pl.when(safe)
    def _():
        safe_gradient(*rest, inv_ref, near_col_ref, grad_ref)

    @pl.when(jnp.logical_not(safe))
    def _():
        col_ref[LINE] = jnp.zeros((2, ROWS, ROWS), jnp.float32)
        fill_columns(col_ref, lambda row: row, near_sent_ref)
        shifted_gradient(*rest, inv_ref, col_ref, grad_ref)

    div = jnp.sum(
        near_sent_ref[DIV_AT : DIV_AT + 1] + sent_ref[DIV_AT : DIV_AT + 1], axis=1, keepdims=True
    ) * (1.0 / (BLOCKS * ROWS))
    high = div.astype(jnp.bfloat16).astype(jnp.float32)
    middle = (div - high).astype(jnp.bfloat16).astype(jnp.float32)
    low = div - high - middle
    lane = lax.broadcasted_iota(jnp.int32, (ROWS, ROWS), 1)
    tail = jnp.where(lane == HEAD, high, jnp.where(lane == HEAD + 1, middle, low))
    for b, out_ref in enumerate(out_refs):
        moved = pltpu.roll(grad_ref[b] * WEIGHT, HEAD, 1)
        out_ref[...] = jnp.where(lane < HEAD, moved, tail).astype(jnp.bfloat16)


def assemble_kernel(*refs):
    in_refs, (grad_ref, div_ref) = refs[:LINE], refs[LINE:]
    x = my_index() >> 3
    lane = lax.broadcasted_iota(jnp.int32, (16, ROWS), 1)
    holds_div = (lane >= HEAD) & (lane < HEAD + 3) & (
        lax.broadcasted_iota(jnp.int32, (16, ROWS), 0) == 0
    )
    for case in range(LINE):

        @pl.when(x == case)
        def _():
            for head in range(LINE):
                from_ref = in_refs[head ^ case]
                grad_ref[:, head * HEAD : head * HEAD + HEAD] = from_ref[:, :HEAD]
                parts = jnp.where(holds_div, from_ref[:16].astype(jnp.float32), 0.0)
                div_ref[head] = jnp.sum(parts)


def shape(*dims, dtype=jnp.bfloat16):
    return jax.ShapeDtypeStruct(dims, dtype)


def call(kernel, name, out_shape, in_specs, out_specs, scratch=(), limit=12 << 20):
    return pl.pallas_call(
        kernel,
        out_shape=out_shape,
        in_specs=in_specs,
        out_specs=out_specs,
        scratch_shapes=list(scratch),
        compiler_params=pltpu.CompilerParams(vmem_limit_bytes=limit),
        name=name,
    )


F32 = jnp.float32
BLOCK_SET = shape(SIDE + 1, ROWS, ROWS)
WIDE_SET = shape(SIDE + 1, ROWS, 2 * ROWS)
ACC = (SIDE + 1, 3, 8, ROWS)
GRAD = (LINE + 1, ROWS, ROWS)
COL = (LINE + 1, 2, ROWS, ROWS)
INV = pltpu.VMEM((2, SIDE + 8, ROWS), F32)


def plan_call(owner_table):
    return call(
        plan_kernel, "list_pairs", shape(PLAN_LEN, dtype=jnp.int32), [SMEM], SMEM, limit=1 << 20
    )(owner_table)


def near_call(plan, half):
    return call(
        near_kernel,
        "near_sums",
        [BLOCK_SET, WIDE_SET, shape(*ACC, dtype=F32)],
        [SMEM, VMEM],
        [VMEM] * 3,
    )(plan, half)


def far_call(plan, other, near_rows, near_wide, near_acc):
    return call(
        far_kernel,
        "far_sums",
        [BLOCK_SET, WIDE_SET, shape(SENT, ROWS, dtype=F32)],
        [SMEM] + [VMEM] * 4,
        [VMEM] * 3,
        [pltpu.VMEM(ACC, F32), pltpu.VMEM((2, SIDE, ROWS), F32)],
    )(plan, other, near_rows, near_wide, near_acc)


def near_grad_call(plan, near_rows, near_wide, near_sent):
    return call(
        near_grad_kernel,
        "near_gradient",
        [shape(*GRAD, dtype=F32), shape(*COL, dtype=F32)],
        [SMEM] + [VMEM] * 3,
        [VMEM] * 2,
        [INV],
    )(plan, near_rows, near_wide, near_sent)


def far_grad_call(*arrays):
    return call(
        far_grad_kernel,
        "far_gradient",
        [shape(ROWS, ROWS)] * LINE,
        [SMEM] + [VMEM] * 7,
        [VMEM] * LINE,
        [INV, pltpu.VMEM(GRAD, F32), pltpu.VMEM(COL, F32)],
    )(*arrays)


def per_device(teacher_q, student_q, owner_table):
    slices = call(
        slice_kernel,
        "slice_heads",
        [shape(ROWS, ROWS)] * LINE,
        [VMEM] * 2,
        [VMEM] * LINE,
        limit=2 << 20,
    )(teacher_q, student_q)
    plan = plan_call(owner_table)
    line = jnp.stack([slices[0]] + [exchanged(slices[b], b << 3) for b in (1, 2, 3)])
    line, plan = lax.optimization_barrier((line, plan))
    half = jnp.concatenate([line] + [exchanged(line, a << 1) for a in (1, 2, 3)])
    other = exchanged(half, 1)
    near_rows, near_wide, near_acc = near_call(plan, half)
    far_rows, far_wide, near_sent = far_call(plan, other, near_rows, near_wide, near_acc)
    far_sent = exchanged(near_sent, 1)
    near_grad, near_col = near_grad_call(plan, near_rows, near_wide, near_sent)
    grads = far_grad_call(
        plan, near_rows, far_rows, far_wide, near_sent, far_sent, near_grad, near_col
    )
    back = [grads[0]] + [exchanged(grads[b], b << 3) for b in (1, 2, 3)]
    return call(
        assemble_kernel,
        "assemble",
        [shape(*teacher_q.shape), shape(LINE, dtype=F32)],
        [VMEM] * LINE,
        [VMEM, SMEM],
        limit=2 << 20,
    )(*back)


def solution(mesh):
    placed = (P("tok", "head"), P("tok", "head"), P())
    return jax.shard_map(
        lambda *arrays: tuple(per_device(*arrays)),
        mesh=mesh,
        in_specs=placed,
        out_specs=(P("tok", "head"), P("head")),
        check_vma=False,
    )
```

```python
import functools

import jax
import jax.numpy as jnp
from jax import lax
from jax.experimental import pallas as pl
from jax.experimental.pallas import tpu as pltpu
from jax.sharding import PartitionSpec as P

HEAD = 64
ROWS = 128
BLOCKS = 32
SIDE = BLOCKS // 2
LINE = 4
LOG2E = 1.4426950408889634
SCALE = HEAD**-0.5
WEIGHT = 32.0 * SCALE
SUM_LIMIT = 2.0**100
FLOOR = -1e30
UNROLL = 16
CHUNK = 4
OWN_UNROLL = 3
PAIRS_AT = 8
OWN_AT = PAIRS_AT + SIDE * SIDE + UNROLL
PLAN_LEN = OWN_AT + LINE * SIDE + CHUNK * OWN_UNROLL + CHUNK
DIV_AT = 2 * SIDE
FLAG_AT = DIV_AT + 1
SENT = DIV_AT + 8
VMEM = pl.BlockSpec(memory_space=pltpu.VMEM)
SMEM = pl.BlockSpec(memory_space=pltpu.SMEM)


def my_index():
    return lax.axis_index("tok")


def exchanged(array, bits):
    return lax.ppermute(array, "tok", [(i, i ^ bits) for i in range(BLOCKS)])


def slice_kernel(teacher_hbm_ref, student_hbm_ref, *refs):
    out_refs, (teacher_ref, student_ref, sem_ref) = refs[:LINE], refs[LINE:]
    copies = [
        pltpu.make_async_copy(teacher_hbm_ref, teacher_ref, sem_ref.at[0]),
        pltpu.make_async_copy(student_hbm_ref, student_ref, sem_ref.at[1]),
    ]
    for copy in copies:
        copy.start()
    for copy in copies:
        copy.wait()
    x = my_index() >> 3
    for head in range(LINE):
        at = slice(head * HEAD, head * HEAD + HEAD)
        both = jnp.concatenate([teacher_ref[:, at], student_ref[:, at]], axis=1)
        for turn, out_ref in enumerate(out_refs):

            @pl.when(x == (head ^ turn))
            def _():
                out_ref[...] = both


def plan_kernel(far, table_hbm_ref, plan_ref, table_ref, sem_ref):
    copy = pltpu.make_async_copy(table_hbm_ref, table_ref, sem_ref)
    copy.start()
    me = my_index()
    core = me & 1
    side = core ^ far
    copy.wait()

    def listed(row, first, prefix):
        inside = [(table_ref[row, 2 * k + side] >= 0).astype(jnp.int32) for k in range(SIDE)]
        at = first
        for k in range(SIDE):
            plan_ref[at] = prefix + k
            at = at + inside[k]
        return at

    def filled(at, count, word):
        for k in range(count):
            plan_ref[at + k] = word

    end = lax.fori_loop(
        0, SIDE, lambda i, at: listed(2 * i + core, at, i * BLOCKS), jnp.int32(PAIRS_AT)
    )
    filled(end, UNROLL, SIDE * BLOCKS)
    plan_ref[0] = end - PAIRS_AT

    def own(b, at):
        end = listed(me ^ (b << 3), at, b * BLOCKS)
        filled(end, CHUNK - 1, b * BLOCKS + SIDE)
        return OWN_AT + (((end - OWN_AT + CHUNK - 1) >> 2) << 2)

    end = lax.fori_loop(0, LINE, own, jnp.int32(OWN_AT))
    filled(end, CHUNK * OWN_UNROLL, LINE * BLOCKS + SIDE)
    plan_ref[1] = (end - OWN_AT) >> 2


def spread(in_ref, rows_ref, wide_ref):
    me = my_index()
    zero = jnp.zeros((HEAD, ROWS), jnp.bfloat16)
    for slot in range(SIDE):
        at = (me >> 1) ^ (((slot & 3) << 2) | (slot >> 2))
        tile = in_ref[slot]
        rows_ref[at] = tile
        flipped = tile.astype(jnp.float32).T.astype(jnp.bfloat16)
        wide_ref[at, :, :ROWS] = jnp.concatenate([flipped[:HEAD], zero], axis=0)
        wide_ref[at, :, ROWS:] = jnp.concatenate([zero, flipped[HEAD:]], axis=0)
    rows_ref[SIDE] = jnp.zeros((ROWS, ROWS), jnp.bfloat16)
    wide_ref[SIDE] = jnp.zeros((ROWS, 2 * ROWS), jnp.bfloat16)


def scores(left, right):
    return jnp.dot(left, right, preferred_element_type=jnp.float32)


def folded(a):
    return jnp.sum(a.reshape(ROWS // 8, 8, ROWS), axis=0)


def totals(exps, raw):
    teacher, student = exps[:, :ROWS], exps[:, ROWS:]
    gap = teacher * (raw[:, :ROWS] - raw[:, ROWS:])
    return folded(teacher), folded(student), folded(gap)


def add_totals(plan_ref, rows_ref, wide_ref, acc_ref):
    pairs = plan_ref[0]

    def turn(group, carry):
        done = []
        for k in range(UNROLL):
            word = plan_ref[PAIRS_AT + group * UNROLL + k]
            row, column = word >> 5, word & (BLOCKS - 1)
            raw = scores(rows_ref[column], wide_ref[row])
            done.append((row, totals(jnp.exp2(raw * (SCALE * LOG2E)), raw)))
        for row, parts in done:
            for k, part in enumerate(parts):
                acc_ref[row, k] += part
        return carry

    lax.fori_loop(0, (pairs + UNROLL - 1) // UNROLL, turn, 0)


def fetched(plan_in_ref, plan_ref, sem_ref):
    copy = pltpu.make_async_copy(plan_in_ref, plan_ref, sem_ref)
    copy.start()
    return copy


def near_kernel(plan_in_ref, half_ref, rows_ref, wide_ref, acc_ref, plan_ref, sem_ref):
    copy = fetched(plan_in_ref, plan_ref, sem_ref)
    spread(half_ref, rows_ref, wide_ref)
    acc_ref[...] = jnp.zeros_like(acc_ref)
    copy.wait()
    add_totals(plan_ref, rows_ref, wide_ref, acc_ref)


def far_kernel(
    near_plan_in_ref,
    plan_in_ref,
    other_ref,
    near_rows_ref,
    near_wide_ref,
    near_acc_ref,
    rows_ref,
    wide_ref,
    sent_ref,
    acc_ref,
    top_ref,
    near_plan_ref,
    near_sem_ref,
    plan_ref,
    sem_ref,
):
    near_copy = fetched(near_plan_in_ref, near_plan_ref, near_sem_ref)
    copy = fetched(plan_in_ref, plan_ref, sem_ref)
    spread(other_ref, rows_ref, wide_ref)
    acc_ref[...] = near_acc_ref[...]
    near_copy.wait()
    copy.wait()
    add_totals(plan_ref, rows_ref, near_wide_ref, acc_ref)

    def row_sums(k):
        return jnp.sum(acc_ref[:SIDE, k], axis=1)

    def finished(teacher_log, student_log, gap_mean, flag):
        sent_ref[:SIDE] = teacher_log
        sent_ref[SIDE : 2 * SIDE] = student_log
        per_row = gap_mean * SCALE - teacher_log + student_log
        row = lax.broadcasted_iota(jnp.int32, (8, ROWS), 0)
        sent_ref[DIV_AT:] = jnp.where(
            row == 0, jnp.sum(per_row, axis=0, keepdims=True), jnp.where(row == 1, flag, 0.0)
        )

    teacher_sum, student_sum, gap_sum = row_sums(0), row_sums(1), row_sums(2)
    fine = (
        (teacher_sum < SUM_LIMIT) & (student_sum < SUM_LIMIT) & (jnp.abs(gap_sum) < SUM_LIMIT)
    )
    safe = jnp.min(fine.astype(jnp.float32)) > 0.5

    @pl.when(safe)
    def _():
        finished(jnp.log(teacher_sum), jnp.log(student_sum), gap_sum / teacher_sum, 0.0)

    @pl.when(jnp.logical_not(safe))
    def _():
        top_ref[...] = jnp.full_like(top_ref, FLOOR)
        acc_ref[...] = jnp.zeros_like(acc_ref)
        lists = ((near_plan_ref, near_rows_ref), (plan_ref, rows_ref))

        def each_pair(act):
            for list_ref, left_ref in lists:

                def turn(n, carry):
                    word = list_ref[PAIRS_AT + n]
                    row, column = word >> 5, word & (BLOCKS - 1)
                    act(row, scores(left_ref[column], near_wide_ref[row]))
                    return carry

                lax.fori_loop(0, list_ref[0], turn, 0)

        def raise_top(row, raw):
            top = jnp.max(raw, axis=0, keepdims=True) * SCALE
            for k in range(2):
                at = (k, pl.ds(row, 1), slice(None))
                top_ref[at] = jnp.maximum(top_ref[at], top[:, k * ROWS : (k + 1) * ROWS])

        def add_shifted(row, raw):
            top = jnp.concatenate([top_ref[k, pl.ds(row, 1), :] for k in range(2)], axis=1)
            for k, part in enumerate(totals(jnp.exp(raw * SCALE - top), raw)):
                acc_ref[row, k] += part

        each_pair(raise_top)
        each_pair(add_shifted)
        teacher_sum, student_sum, gap_sum = row_sums(0), row_sums(1), row_sums(2)
        finished(
            top_ref[0] + jnp.log(teacher_sum),
            top_ref[1] + jnp.log(student_sum),
            gap_sum / teacher_sum,
            1.0,
        )


def along_rows(row):
    return jnp.broadcast_to(row, (ROWS, ROWS)).T


def own_at(b):
    return (my_index() >> 1) ^ ((b & 3) << 2)


def is_safe(sent_ref):
    return jnp.max(sent_ref[FLAG_AT : FLAG_AT + 1]) < 0.5


def fill_columns(col_ref, value, near_sent_ref):
    for b in range(LINE):
        for k in range(2):
            row = near_sent_ref[pl.ds(own_at(b) + k * SIDE, 1), :]
            col_ref[b, k] = along_rows(value(row))


def safe_gradient(
    plan_ref, near_rows_ref, rows_ref, wide_ref, sent_ref, inv_ref, col_ref, grad_ref, copy
):
    inv_ref[...] = jnp.zeros_like(inv_ref)
    for k in range(2):
        inv_ref[k, :SIDE] = jnp.exp(-sent_ref[k * SIDE : (k + 1) * SIDE])
    copy.wait()
    chunks = plan_ref[1]

    def chunk_part(at):
        words = [plan_ref[at + k] for k in range(CHUNK)]
        b = words[0] >> 5
        columns = [w & (BLOCKS - 1) for w in words]
        wide = jnp.concatenate([wide_ref[c] for c in columns], axis=1)
        exps = jnp.exp2(scores(near_rows_ref[own_at(b)], wide) * (SCALE * LOG2E))
        symmetric = []
        for k, c in enumerate(columns):
            at_k = 2 * ROWS * k
            teacher, student = exps[:, at_k : at_k + ROWS], exps[:, at_k + ROWS : at_k + 2 * ROWS]
            teacher_inv = col_ref[b, 0] + inv_ref[0, pl.ds(c, 1), :]
            student_inv = col_ref[b, 1] + inv_ref[1, pl.ds(c, 1), :]
            symmetric.append((student * student_inv - teacher * teacher_inv).astype(jnp.bfloat16))
        right = jnp.concatenate([rows_ref[c] for c in columns], axis=0)
        return b, scores(jnp.concatenate(symmetric, axis=1), right)

    def turn(group, carry):
        done = [
            chunk_part(OWN_AT + (group * OWN_UNROLL + k) * CHUNK) for k in range(OWN_UNROLL)
        ]
        for b, part in done:
            grad_ref[b] += part
        return carry

    lax.fori_loop(0, (chunks + OWN_UNROLL - 1) // OWN_UNROLL, turn, 0)


def shifted_gradient(
    plan_ref, near_rows_ref, rows_ref, wide_ref, sent_ref, inv_ref, col_ref, grad_ref, copy
):
    inv_ref[...] = jnp.zeros_like(inv_ref)
    for k in range(2):
        inv_ref[k, :SIDE] = sent_ref[k * SIDE : (k + 1) * SIDE]
    copy.wait()
    chunks = plan_ref[1]

    def turn(n, carry):
        word = plan_ref[OWN_AT + n]
        b, c = word >> 5, word & (BLOCKS - 1)

        @pl.when(c < SIDE)
        def _():
            raw = scores(near_rows_ref[own_at(b)], wide_ref[c]) * SCALE
            teacher, student = raw[:, :ROWS], raw[:, ROWS:]
            row_gap = jnp.exp(student - col_ref[b, 1]) - jnp.exp(teacher - col_ref[b, 0])
            column_gap = jnp.exp(student - inv_ref[1, pl.ds(c, 1), :]) - jnp.exp(
                teacher - inv_ref[0, pl.ds(c, 1), :]
            )
            grad_ref[b] += scores((row_gap + column_gap).astype(jnp.bfloat16), rows_ref[c])

        return carry

    lax.fori_loop(0, chunks * CHUNK, turn, 0)


def near_grad_kernel(
    plan_in_ref, rows_ref, wide_ref, sent_ref, grad_ref, col_ref, inv_ref, plan_ref, sem_ref
):
    copy = fetched(plan_in_ref, plan_ref, sem_ref)
    grad_ref[...] = jnp.zeros_like(grad_ref)
    col_ref[LINE] = jnp.zeros((2, ROWS, ROWS), jnp.float32)
    rest = (plan_ref, rows_ref, rows_ref, wide_ref, sent_ref)
    safe = is_safe(sent_ref)

    @pl.when(safe)
    def _():
        fill_columns(col_ref, lambda row: jnp.exp(-row), sent_ref)
        safe_gradient(*rest, inv_ref, col_ref, grad_ref, copy)

    @pl.when(jnp.logical_not(safe))
    def _():
        fill_columns(col_ref, lambda row: row, sent_ref)
        shifted_gradient(*rest, inv_ref, col_ref, grad_ref, copy)


def far_grad_kernel(
    plan_in_ref,
    near_rows_ref,
    rows_ref,
    wide_ref,
    near_sent_ref,
    sent_ref,
    near_grad_ref,
    near_col_ref,
    *refs,
):
    out_refs, (inv_ref, grad_ref, col_ref, plan_ref, sem_ref) = refs[:LINE], refs[LINE:]
    copy = fetched(plan_in_ref, plan_ref, sem_ref)
    grad_ref[...] = near_grad_ref[...]
    rest = (plan_ref, near_rows_ref, rows_ref, wide_ref, sent_ref)
    safe = is_safe(sent_ref) & is_safe(near_sent_ref)

    @pl.when(safe)
    def _():
        safe_gradient(*rest, inv_ref, near_col_ref, grad_ref, copy)

    @pl.when(jnp.logical_not(safe))
    def _():
        col_ref[LINE] = jnp.zeros((2, ROWS, ROWS), jnp.float32)
        fill_columns(col_ref, lambda row: row, near_sent_ref)
        shifted_gradient(*rest, inv_ref, col_ref, grad_ref, copy)

    div = jnp.sum(
        near_sent_ref[DIV_AT : DIV_AT + 1] + sent_ref[DIV_AT : DIV_AT + 1], axis=1, keepdims=True
    ) * (1.0 / (BLOCKS * ROWS))
    high = div.astype(jnp.bfloat16).astype(jnp.float32)
    middle = (div - high).astype(jnp.bfloat16).astype(jnp.float32)
    low = div - high - middle
    lane = lax.broadcasted_iota(jnp.int32, (ROWS, ROWS), 1)
    tail = jnp.where(lane == HEAD, high, jnp.where(lane == HEAD + 1, middle, low))
    for b, out_ref in enumerate(out_refs):
        moved = pltpu.roll(grad_ref[b] * WEIGHT, HEAD, 1)
        out_ref[...] = jnp.where(lane < HEAD, moved, tail).astype(jnp.bfloat16)


def assemble_kernel(*refs):
    in_refs, (grad_ref, div_ref) = refs[:LINE], refs[LINE:]
    x = my_index() >> 3
    lane = lax.broadcasted_iota(jnp.int32, (16, ROWS), 1)
    holds_div = (lane >= HEAD) & (lane < HEAD + 3) & (
        lax.broadcasted_iota(jnp.int32, (16, ROWS), 0) == 0
    )
    for case in range(LINE):

        @pl.when(x == case)
        def _():
            for head in range(LINE):
                from_ref = in_refs[head ^ case]
                grad_ref[:, head * HEAD : head * HEAD + HEAD] = from_ref[:, :HEAD]
                parts = jnp.where(holds_div, from_ref[:16].astype(jnp.float32), 0.0)
                div_ref[head] = jnp.sum(parts)


def shape(*dims, dtype=jnp.bfloat16):
    return jax.ShapeDtypeStruct(dims, dtype)


def call(kernel, name, out_shape, in_specs, out_specs, scratch=(), limit=12 << 20):
    return pl.pallas_call(
        kernel,
        out_shape=out_shape,
        in_specs=in_specs,
        out_specs=out_specs,
        scratch_shapes=list(scratch),
        compiler_params=pltpu.CompilerParams(vmem_limit_bytes=limit),
        name=name,
    )


F32 = jnp.float32
BLOCK_SET = shape(SIDE + 1, ROWS, ROWS)
WIDE_SET = shape(SIDE + 1, ROWS, 2 * ROWS)
ACC = (SIDE + 1, 3, 8, ROWS)
GRAD = (LINE + 1, ROWS, ROWS)
COL = (LINE + 1, 2, ROWS, ROWS)
INV = pltpu.VMEM((2, SIDE + 8, ROWS), F32)
PLAN = [pltpu.SMEM((PLAN_LEN,), jnp.int32), pltpu.SemaphoreType.DMA]


def plan_call(owner_table, far):
    return call(
        functools.partial(plan_kernel, far),
        ("list_near_pairs", "list_far_pairs")[far],
        shape(PLAN_LEN, dtype=jnp.int32),
        [pl.BlockSpec(memory_space=pltpu.HBM)],
        SMEM,
        [pltpu.SMEM((BLOCKS, BLOCKS), jnp.int32), pltpu.SemaphoreType.DMA],
        limit=1 << 20,
    )(pltpu.with_memory_space_constraint(owner_table, pltpu.HBM))


def near_call(plan, half):
    return call(
        near_kernel,
        "near_sums",
        [BLOCK_SET, WIDE_SET, shape(*ACC, dtype=F32)],
        [VMEM] * 2,
        [VMEM] * 3,
        PLAN,
    )(plan, half)


def far_call(near_plan, plan, other, near_rows, near_wide, near_acc):
    return call(
        far_kernel,
        "far_sums",
        [BLOCK_SET, WIDE_SET, shape(SENT, ROWS, dtype=F32)],
        [VMEM] * 6,
        [VMEM] * 3,
        [pltpu.VMEM(ACC, F32), pltpu.VMEM((2, SIDE, ROWS), F32), *PLAN, *PLAN],
    )(near_plan, plan, other, near_rows, near_wide, near_acc)


def near_grad_call(plan, near_rows, near_wide, near_sent):
    return call(
        near_grad_kernel,
        "near_gradient",
        [shape(*GRAD, dtype=F32), shape(*COL, dtype=F32)],
        [VMEM] * 4,
        [VMEM] * 2,
        [INV, *PLAN],
    )(plan, near_rows, near_wide, near_sent)


def far_grad_call(*arrays):
    return call(
        far_grad_kernel,
        "far_gradient",
        [shape(ROWS, ROWS)] * LINE,
        [VMEM] * 8,
        [VMEM] * LINE,
        [INV, pltpu.VMEM(GRAD, F32), pltpu.VMEM(COL, F32), *PLAN],
    )(*arrays)


def per_device(teacher_q, student_q, owner_table):
    slices = call(
        slice_kernel,
        "slice_heads",
        [shape(ROWS, ROWS)] * LINE,
        [pl.BlockSpec(memory_space=pltpu.HBM)] * 2,
        [VMEM] * LINE,
        [pltpu.VMEM(teacher_q.shape, jnp.bfloat16)] * 2 + [pltpu.SemaphoreType.DMA((2,))],
        limit=2 << 20,
    )(*[pltpu.with_memory_space_constraint(a, pltpu.HBM) for a in (teacher_q, student_q)])
    near_plan, far_plan = plan_call(owner_table, 0), plan_call(owner_table, 1)
    line = jnp.stack([slices[0]] + [exchanged(slices[b], b << 3) for b in (1, 2, 3)])
    line, near_plan = lax.optimization_barrier((line, near_plan))
    half = jnp.concatenate([line] + [exchanged(line, a << 1) for a in (1, 2, 3)])
    half, far_plan = lax.optimization_barrier((half, far_plan))
    other = exchanged(half, 1)
    near_rows, near_wide, near_acc = near_call(near_plan, half)
    far_rows, far_wide, near_sent = far_call(
        near_plan, far_plan, other, near_rows, near_wide, near_acc
    )
    far_sent = exchanged(near_sent, 1)
    near_grad, near_col = near_grad_call(near_plan, near_rows, near_wide, near_sent)
    grads = far_grad_call(
        far_plan, near_rows, far_rows, far_wide, near_sent, far_sent, near_grad, near_col
    )
    back = [grads[0]] + [exchanged(grads[b], b << 3) for b in (1, 2, 3)]
    return call(
        assemble_kernel,
        "assemble",
        [shape(*teacher_q.shape), shape(LINE, dtype=F32)],
        [VMEM] * LINE,
        [VMEM, SMEM],
        limit=2 << 20,
    )(*back)


def solution(mesh):
    placed = (P("tok", "head"), P("tok", "head"), P())
    return jax.shard_map(
        lambda *arrays: tuple(per_device(*arrays)),
        mesh=mesh,
        in_specs=placed,
        out_specs=(P("tok", "head"), P("head")),
        check_vma=False,
    )
```

```python
import functools

import jax
import jax.numpy as jnp
from jax import lax
from jax.experimental import pallas as pl
from jax.experimental.pallas import tpu as pltpu
from jax.sharding import PartitionSpec as P

HEAD = 64
ROWS = 128
BLOCKS = 32
SIDE = BLOCKS // 2
LINE = 4
LOG2E = 1.4426950408889634
SCALE = HEAD**-0.5
WEIGHT = 32.0 * SCALE
SUM_LIMIT = 2.0**100
FLOOR = -1e30
UNROLL = 16
CHUNK = 4
OWN_UNROLL = 8
PAIRS_AT = 8
OWN_AT = PAIRS_AT + SIDE * SIDE + UNROLL
PLAN_LEN = OWN_AT + LINE * SIDE + CHUNK * OWN_UNROLL + CHUNK
DIV_AT = 2 * SIDE
FLAG_AT = DIV_AT + 1
SENT = DIV_AT + 8
VMEM = pl.BlockSpec(memory_space=pltpu.VMEM)
SMEM = pl.BlockSpec(memory_space=pltpu.SMEM)


def my_index():
    return lax.axis_index("tok")


def met(k):
    return (0, 3, 2, 1)[k]


def exchanged(array, code, shift):
    return lax.ppermute(array, "tok", [(i, i ^ (code << shift)) for i in range(BLOCKS)])


def swapped(array):
    return lax.ppermute(array, "tok", [(i, i ^ 1) for i in range(BLOCKS)])


def slice_kernel(teacher_hbm_ref, student_hbm_ref, *refs):
    out_refs, (teacher_ref, student_ref, sem_ref) = refs[:LINE], refs[LINE:]
    copies = [
        pltpu.make_async_copy(teacher_hbm_ref, teacher_ref, sem_ref.at[0]),
        pltpu.make_async_copy(student_hbm_ref, student_ref, sem_ref.at[1]),
    ]
    for copy in copies:
        copy.start()
    for copy in copies:
        copy.wait()
    me = my_index()
    for head in range(LINE):
        at = slice(head * HEAD, head * HEAD + HEAD)
        both = jnp.concatenate([teacher_ref[:, at], student_ref[:, at]], axis=1)
        for turn, out_ref in enumerate(out_refs):

            @pl.when((me >> 3) == (head ^ met(turn)))
            def _():
                out_ref[...] = both


def plan_kernel(far, table_hbm_ref, plan_ref, table_ref, sem_ref):
    copy = pltpu.make_async_copy(table_hbm_ref, table_ref, sem_ref)
    copy.start()
    me = my_index()
    core = me & 1
    side = core ^ far
    copy.wait()

    def listed(row, first, prefix):
        inside = [(table_ref[row, 2 * k + side] >= 0).astype(jnp.int32) for k in range(SIDE)]
        at = first
        for k in range(SIDE):
            plan_ref[at] = prefix + k
            at = at + inside[k]
        return at

    def filled(at, count, word):
        for k in range(count):
            plan_ref[at + k] = word

    end = lax.fori_loop(
        0, SIDE, lambda i, at: listed(2 * i + core, at, i * BLOCKS), jnp.int32(PAIRS_AT)
    )
    filled(end, UNROLL, SIDE * BLOCKS)
    plan_ref[0] = end - PAIRS_AT

    def own(b, at):
        end = listed(me ^ (b << 3), at, b * BLOCKS)
        filled(end, CHUNK - 1, b * BLOCKS + SIDE)
        return OWN_AT + (end - OWN_AT + CHUNK - 1) // CHUNK * CHUNK

    end = lax.fori_loop(0, LINE, own, jnp.int32(OWN_AT))
    filled(end, CHUNK * OWN_UNROLL, LINE * BLOCKS + SIDE)
    plan_ref[1] = (end - OWN_AT) // CHUNK


def spread(in_ref, rows_ref, wide_ref):
    me = my_index()
    zero = jnp.zeros((HEAD, ROWS), jnp.bfloat16)
    for slot in range(SIDE):
        at = (me >> 1) ^ ((met(slot & 3) << 2) | (slot >> 2))
        tile = in_ref[slot]
        rows_ref[at] = tile
        flipped = tile.astype(jnp.float32).T.astype(jnp.bfloat16)
        wide_ref[at, :, :ROWS] = jnp.concatenate([flipped[:HEAD], zero], axis=0)
        wide_ref[at, :, ROWS:] = jnp.concatenate([zero, flipped[HEAD:]], axis=0)
    rows_ref[SIDE] = jnp.zeros((ROWS, ROWS), jnp.bfloat16)
    wide_ref[SIDE] = jnp.zeros((ROWS, 2 * ROWS), jnp.bfloat16)


def scores(left, right):
    return jnp.dot(left, right, preferred_element_type=jnp.float32)


def folded(a):
    return jnp.sum(a.reshape(ROWS // 8, 8, ROWS), axis=0)


def totals(exps, raw):
    teacher, student = exps[:, :ROWS], exps[:, ROWS:]
    gap = teacher * (raw[:, :ROWS] - raw[:, ROWS:])
    return folded(teacher), folded(student), folded(gap)


def add_totals(plan_ref, rows_ref, wide_ref, acc_ref):
    pairs = plan_ref[0]

    def turn(first, count):
        done = []
        for k in range(count):
            word = plan_ref[first + k]
            row, column = word >> 5, word & (BLOCKS - 1)
            raw = scores(rows_ref[column], wide_ref[row])
            done.append((row, totals(jnp.exp2(raw * (SCALE * LOG2E)), raw)))
        for row, parts in done:
            for k, part in enumerate(parts):
                acc_ref[row, k] += part
        return 0

    long = pairs // (2 * UNROLL)
    lax.fori_loop(0, long, lambda n, c: turn(PAIRS_AT + n * 2 * UNROLL, 2 * UNROLL), 0)
    rest = pairs - long * 2 * UNROLL
    lax.fori_loop(
        0,
        (rest + UNROLL - 1) // UNROLL,
        lambda n, c: turn(PAIRS_AT + (2 * long + n) * UNROLL, UNROLL),
        0,
    )


def fetched(plan_in_ref, plan_ref, sem_ref):
    copy = pltpu.make_async_copy(plan_in_ref, plan_ref, sem_ref)
    copy.start()
    return copy


def near_kernel(plan_in_ref, half_ref, rows_ref, wide_ref, acc_ref, plan_ref, sem_ref):
    copy = fetched(plan_in_ref, plan_ref, sem_ref)
    spread(half_ref, rows_ref, wide_ref)
    acc_ref[...] = jnp.zeros_like(acc_ref)
    copy.wait()
    add_totals(plan_ref, rows_ref, wide_ref, acc_ref)


def far_kernel(
    near_plan_in_ref,
    plan_in_ref,
    other_ref,
    near_rows_ref,
    near_wide_ref,
    near_acc_ref,
    rows_ref,
    wide_ref,
    sent_ref,
    acc_ref,
    top_ref,
    near_plan_ref,
    near_sem_ref,
    plan_ref,
    sem_ref,
):
    near_copy = fetched(near_plan_in_ref, near_plan_ref, near_sem_ref)
    copy = fetched(plan_in_ref, plan_ref, sem_ref)
    spread(other_ref, rows_ref, wide_ref)
    acc_ref[...] = near_acc_ref[...]
    near_copy.wait()
    copy.wait()
    add_totals(plan_ref, rows_ref, near_wide_ref, acc_ref)

    def row_sums(k):
        return jnp.sum(acc_ref[:SIDE, k], axis=1)

    def finished(teacher_log, student_log, gap_mean, flag):
        sent_ref[:SIDE] = teacher_log
        sent_ref[SIDE : 2 * SIDE] = student_log
        per_row = gap_mean * SCALE - teacher_log + student_log
        row = lax.broadcasted_iota(jnp.int32, (8, ROWS), 0)
        sent_ref[DIV_AT:] = jnp.where(
            row == 0, jnp.sum(per_row, axis=0, keepdims=True), jnp.where(row == 1, flag, 0.0)
        )

    teacher_sum, student_sum, gap_sum = row_sums(0), row_sums(1), row_sums(2)
    fine = (
        (teacher_sum < SUM_LIMIT) & (student_sum < SUM_LIMIT) & (jnp.abs(gap_sum) < SUM_LIMIT)
    )
    safe = jnp.min(fine.astype(jnp.float32)) > 0.5

    @pl.when(safe)
    def _():
        finished(jnp.log(teacher_sum), jnp.log(student_sum), gap_sum / teacher_sum, 0.0)

    @pl.when(jnp.logical_not(safe))
    def _():
        top_ref[...] = jnp.full_like(top_ref, FLOOR)
        acc_ref[...] = jnp.zeros_like(acc_ref)
        lists = ((near_plan_ref, near_rows_ref), (plan_ref, rows_ref))

        def each_pair(act):
            for list_ref, left_ref in lists:

                def turn(n, carry):
                    word = list_ref[PAIRS_AT + n]
                    row, column = word >> 5, word & (BLOCKS - 1)
                    act(row, scores(left_ref[column], near_wide_ref[row]))
                    return carry

                lax.fori_loop(0, list_ref[0], turn, 0)

        def raise_top(row, raw):
            top = jnp.max(raw, axis=0, keepdims=True) * SCALE
            for k in range(2):
                at = (k, pl.ds(row, 1), slice(None))
                top_ref[at] = jnp.maximum(top_ref[at], top[:, k * ROWS : (k + 1) * ROWS])

        def add_shifted(row, raw):
            top = jnp.concatenate([top_ref[k, pl.ds(row, 1), :] for k in range(2)], axis=1)
            for k, part in enumerate(totals(jnp.exp(raw * SCALE - top), raw)):
                acc_ref[row, k] += part

        each_pair(raise_top)
        each_pair(add_shifted)
        teacher_sum, student_sum, gap_sum = row_sums(0), row_sums(1), row_sums(2)
        finished(
            top_ref[0] + jnp.log(teacher_sum),
            top_ref[1] + jnp.log(student_sum),
            gap_sum / teacher_sum,
            1.0,
        )


def along_rows(row):
    return jnp.broadcast_to(row, (ROWS, ROWS)).T


def own_at(b):
    return (my_index() >> 1) ^ ((b & 3) << 2)


def is_safe(sent_ref):
    return jnp.max(sent_ref[FLAG_AT : FLAG_AT + 1]) < 0.5


def fill_columns(col_ref, value, near_sent_ref):
    for b in range(LINE):
        for k in range(2):
            row = near_sent_ref[pl.ds(own_at(b) + k * SIDE, 1), :]
            col_ref[b, k] = along_rows(value(row))


def safe_gradient(
    plan_ref, near_rows_ref, rows_ref, wide_ref, sent_ref, inv_ref, col_ref, grad_ref, copy
):
    inv_ref[...] = jnp.zeros_like(inv_ref)
    for k in range(2):
        inv_ref[k, :SIDE] = jnp.exp(-sent_ref[k * SIDE : (k + 1) * SIDE])
    copy.wait()
    chunks = plan_ref[1]

    def turn(group, carry):
        words = [
            [plan_ref[OWN_AT + (group * OWN_UNROLL + k) * CHUNK + n] for n in range(CHUNK)]
            for k in range(OWN_UNROLL)
        ]
        owns = [chunk[0] >> 5 for chunk in words]
        columns = [[w & (BLOCKS - 1) for w in chunk] for chunk in words]
        raws = [
            scores(
                near_rows_ref[own_at(b)], jnp.concatenate([wide_ref[c] for c in chunk], axis=1)
            )
            for b, chunk in zip(owns, columns)
        ]
        symmetric = []
        for b, chunk, raw in zip(owns, columns, raws):
            parts = []
            for n, c in enumerate(chunk):
                exps = jnp.exp2(raw[:, 2 * ROWS * n : 2 * ROWS * (n + 1)] * (SCALE * LOG2E))
                teacher_inv = col_ref[b, 0] + inv_ref[0, pl.ds(c, 1), :]
                student_inv = col_ref[b, 1] + inv_ref[1, pl.ds(c, 1), :]
                gap = exps[:, ROWS:] * student_inv - exps[:, :ROWS] * teacher_inv
                parts.append(gap.astype(jnp.bfloat16))
            symmetric.append(jnp.concatenate(parts, axis=1))
        done = [
            (b, scores(sym, jnp.concatenate([rows_ref[c] for c in chunk], axis=0)))
            for b, chunk, sym in zip(owns, columns, symmetric)
        ]
        for b, part in done:
            grad_ref[b] += part
        return carry

    lax.fori_loop(0, (chunks + OWN_UNROLL - 1) // OWN_UNROLL, turn, 0)


def shifted_gradient(
    plan_ref, near_rows_ref, rows_ref, wide_ref, sent_ref, inv_ref, col_ref, grad_ref, copy
):
    inv_ref[...] = jnp.zeros_like(inv_ref)
    for k in range(2):
        inv_ref[k, :SIDE] = sent_ref[k * SIDE : (k + 1) * SIDE]
    copy.wait()
    chunks = plan_ref[1]

    def turn(n, carry):
        word = plan_ref[OWN_AT + n]
        b, c = word >> 5, word & (BLOCKS - 1)

        @pl.when(c < SIDE)
        def _():
            raw = scores(near_rows_ref[own_at(b)], wide_ref[c]) * SCALE
            teacher, student = raw[:, :ROWS], raw[:, ROWS:]
            row_gap = jnp.exp(student - col_ref[b, 1]) - jnp.exp(teacher - col_ref[b, 0])
            column_gap = jnp.exp(student - inv_ref[1, pl.ds(c, 1), :]) - jnp.exp(
                teacher - inv_ref[0, pl.ds(c, 1), :]
            )
            grad_ref[b] += scores((row_gap + column_gap).astype(jnp.bfloat16), rows_ref[c])

        return carry

    lax.fori_loop(0, chunks * CHUNK, turn, 0)


def near_grad_kernel(
    plan_in_ref, rows_ref, wide_ref, sent_ref, grad_ref, col_ref, inv_ref, plan_ref, sem_ref
):
    copy = fetched(plan_in_ref, plan_ref, sem_ref)
    grad_ref[...] = jnp.zeros_like(grad_ref)
    col_ref[LINE] = jnp.zeros((2, ROWS, ROWS), jnp.float32)
    rest = (plan_ref, rows_ref, rows_ref, wide_ref, sent_ref)
    safe = is_safe(sent_ref)

    @pl.when(safe)
    def _():
        fill_columns(col_ref, lambda row: jnp.exp(-row), sent_ref)
        safe_gradient(*rest, inv_ref, col_ref, grad_ref, copy)

    @pl.when(jnp.logical_not(safe))
    def _():
        fill_columns(col_ref, lambda row: row, sent_ref)
        shifted_gradient(*rest, inv_ref, col_ref, grad_ref, copy)


def far_grad_kernel(
    plan_in_ref,
    near_rows_ref,
    rows_ref,
    wide_ref,
    near_sent_ref,
    sent_ref,
    near_grad_ref,
    near_col_ref,
    *refs,
):
    out_refs, (inv_ref, grad_ref, col_ref, plan_ref, sem_ref) = refs[:LINE], refs[LINE:]
    copy = fetched(plan_in_ref, plan_ref, sem_ref)
    grad_ref[...] = near_grad_ref[...]
    rest = (plan_ref, near_rows_ref, rows_ref, wide_ref, sent_ref)
    safe = is_safe(sent_ref) & is_safe(near_sent_ref)

    @pl.when(safe)
    def _():
        safe_gradient(*rest, inv_ref, near_col_ref, grad_ref, copy)

    @pl.when(jnp.logical_not(safe))
    def _():
        col_ref[LINE] = jnp.zeros((2, ROWS, ROWS), jnp.float32)
        fill_columns(col_ref, lambda row: row, near_sent_ref)
        shifted_gradient(*rest, inv_ref, col_ref, grad_ref, copy)

    div = jnp.sum(
        near_sent_ref[DIV_AT : DIV_AT + 1] + sent_ref[DIV_AT : DIV_AT + 1], axis=1, keepdims=True
    ) * (1.0 / (BLOCKS * ROWS))
    high = div.astype(jnp.bfloat16).astype(jnp.float32)
    middle = (div - high).astype(jnp.bfloat16).astype(jnp.float32)
    low = div - high - middle
    lane = lax.broadcasted_iota(jnp.int32, (ROWS, ROWS), 1)
    tail = jnp.where(lane == HEAD, high, jnp.where(lane == HEAD + 1, middle, low))
    for k, out_ref in enumerate(out_refs):
        moved = pltpu.roll(grad_ref[met(k)] * WEIGHT, HEAD, 1)
        out_ref[...] = jnp.where(lane < HEAD, moved, tail).astype(jnp.bfloat16)


def assemble_kernel(*refs):
    in_refs, (grad_ref, div_ref) = refs[:LINE], refs[LINE:]
    x = my_index() >> 3
    lane = lax.broadcasted_iota(jnp.int32, (16, ROWS), 1)
    holds_div = (lane >= HEAD) & (lane < HEAD + 3) & (
        lax.broadcasted_iota(jnp.int32, (16, ROWS), 0) == 0
    )
    for case in range(LINE):

        @pl.when(x == case)
        def _():
            for head in range(LINE):
                from_ref = in_refs[met(head ^ case)]
                grad_ref[:, head * HEAD : head * HEAD + HEAD] = from_ref[:, :HEAD]
                parts = jnp.where(holds_div, from_ref[:16].astype(jnp.float32), 0.0)
                div_ref[head] = jnp.sum(parts)


def shape(*dims, dtype=jnp.bfloat16):
    return jax.ShapeDtypeStruct(dims, dtype)


def call(kernel, name, out_shape, in_specs, out_specs, scratch=(), limit=12 << 20):
    return pl.pallas_call(
        kernel,
        out_shape=out_shape,
        in_specs=in_specs,
        out_specs=out_specs,
        scratch_shapes=list(scratch),
        compiler_params=pltpu.CompilerParams(vmem_limit_bytes=limit),
        name=name,
    )


F32 = jnp.float32
BLOCK_SET = shape(SIDE + 1, ROWS, ROWS)
WIDE_SET = shape(SIDE + 1, ROWS, 2 * ROWS)
ACC = (SIDE + 1, 3, 8, ROWS)
GRAD = (LINE + 1, ROWS, ROWS)
COL = (LINE + 1, 2, ROWS, ROWS)
INV = pltpu.VMEM((2, SIDE + 8, ROWS), F32)
PLAN = [pltpu.SMEM((PLAN_LEN,), jnp.int32), pltpu.SemaphoreType.DMA]


def plan_call(owner_table, far):
    return call(
        functools.partial(plan_kernel, far),
        ("list_near_pairs", "list_far_pairs")[far],
        shape(PLAN_LEN, dtype=jnp.int32),
        [pl.BlockSpec(memory_space=pltpu.HBM)],
        SMEM,
        [pltpu.SMEM((BLOCKS, BLOCKS), jnp.int32), pltpu.SemaphoreType.DMA],
        limit=1 << 20,
    )(pltpu.with_memory_space_constraint(owner_table, pltpu.HBM))


def near_call(plan, half):
    return call(
        near_kernel,
        "near_sums",
        [BLOCK_SET, WIDE_SET, shape(*ACC, dtype=F32)],
        [VMEM] * 2,
        [VMEM] * 3,
        PLAN,
    )(plan, half)


def far_call(near_plan, plan, other, near_rows, near_wide, near_acc):
    return call(
        far_kernel,
        "far_sums",
        [BLOCK_SET, WIDE_SET, shape(SENT, ROWS, dtype=F32)],
        [VMEM] * 6,
        [VMEM] * 3,
        [pltpu.VMEM(ACC, F32), pltpu.VMEM((2, SIDE, ROWS), F32), *PLAN, *PLAN],
    )(near_plan, plan, other, near_rows, near_wide, near_acc)


def near_grad_call(plan, near_rows, near_wide, near_sent):
    return call(
        near_grad_kernel,
        "near_gradient",
        [shape(*GRAD, dtype=F32), shape(*COL, dtype=F32)],
        [VMEM] * 4,
        [VMEM] * 2,
        [INV, *PLAN],
    )(plan, near_rows, near_wide, near_sent)


def far_grad_call(*arrays):
    return call(
        far_grad_kernel,
        "far_gradient",
        [shape(ROWS, ROWS)] * LINE,
        [VMEM] * 8,
        [VMEM] * LINE,
        [INV, pltpu.VMEM(GRAD, F32), pltpu.VMEM(COL, F32), *PLAN],
    )(*arrays)


def per_device(teacher_q, student_q, owner_table):
    slices = call(
        slice_kernel,
        "slice_heads",
        [shape(ROWS, ROWS)] * LINE,
        [pl.BlockSpec(memory_space=pltpu.HBM)] * 2,
        [VMEM] * LINE,
        [pltpu.VMEM(teacher_q.shape, jnp.bfloat16)] * 2 + [pltpu.SemaphoreType.DMA((2,))],
        limit=2 << 20,
    )(*[pltpu.with_memory_space_constraint(a, pltpu.HBM) for a in (teacher_q, student_q)])
    near_plan, far_plan = plan_call(owner_table, 0), plan_call(owner_table, 1)
    line = jnp.stack([slices[0]] + [exchanged(slices[b], met(b), 3) for b in (1, 2, 3)])
    line, near_plan = lax.optimization_barrier((line, near_plan))
    half = jnp.concatenate([line] + [exchanged(line, a, 1) for a in (1, 2, 3)])
    half, far_plan = lax.optimization_barrier((half, far_plan))
    other = swapped(half)
    near_rows, near_wide, near_acc = near_call(near_plan, half)
    far_rows, far_wide, near_sent = far_call(
        near_plan, far_plan, other, near_rows, near_wide, near_acc
    )
    far_sent = swapped(near_sent)
    near_grad, near_col = near_grad_call(near_plan, near_rows, near_wide, near_sent)
    grads = far_grad_call(
        far_plan, near_rows, far_rows, far_wide, near_sent, far_sent, near_grad, near_col
    )
    back = [grads[0]] + [exchanged(grads[b], met(b), 3) for b in (1, 2, 3)]
    return call(
        assemble_kernel,
        "assemble",
        [shape(*teacher_q.shape), shape(LINE, dtype=F32)],
        [VMEM] * LINE,
        [VMEM, SMEM],
        limit=2 << 20,
    )(*back)


def solution(mesh):
    placed = (P("tok", "head"), P("tok", "head"), P())
    return jax.shard_map(
        lambda *arrays: tuple(per_device(*arrays)),
        mesh=mesh,
        in_specs=placed,
        out_specs=(P("tok", "head"), P("head")),
        check_vma=False,
    )
```

```python
import functools

import jax
import jax.numpy as jnp
from jax import lax
from jax.experimental import pallas as pl
from jax.experimental.pallas import tpu as pltpu
from jax.sharding import PartitionSpec as P

HEAD = 64
ROWS = 128
HALF = ROWS // 2
BLOCKS = 32
SIDE = BLOCKS // 2
LINE = 4
LOG2E = 1.4426950408889634
SCALE = HEAD**-0.5
WEIGHT = 32.0 * SCALE
SUM_LIMIT = 2.0**100
FLOOR = -1e30
UNROLL = 16
CHUNK = 4
OWN_UNROLL = 8
PAIRS_AT = 8
OWN_AT = PAIRS_AT + SIDE * SIDE + UNROLL
PLAN_LEN = OWN_AT + LINE * SIDE + CHUNK * OWN_UNROLL + CHUNK
DIV_AT = 2 * SIDE
FLAG_AT = DIV_AT + 1
SENT = DIV_AT + 8
VMEM = pl.BlockSpec(memory_space=pltpu.VMEM)
SMEM = pl.BlockSpec(memory_space=pltpu.SMEM)


def my_index():
    return lax.axis_index("tok")


MET_X = (0, 3, 2, 1)
MET_Y = (0, 1, 3, 2)
MET_BACK = (0, 2, 3, 1)


def exchanged(array, code, shift):
    return lax.ppermute(array, "tok", [(i, i ^ (code << shift)) for i in range(BLOCKS)])


def swapped(array):
    return lax.ppermute(array, "tok", [(i, i ^ 1) for i in range(BLOCKS)])


def slice_kernel(teacher_hbm_ref, student_hbm_ref, *refs):
    out_refs, (teacher_ref, student_ref, sem_ref) = refs[:LINE], refs[LINE:]
    copies = [
        pltpu.make_async_copy(teacher_hbm_ref, teacher_ref, sem_ref.at[0]),
        pltpu.make_async_copy(student_hbm_ref, student_ref, sem_ref.at[1]),
    ]
    for copy in copies:
        copy.start()
    for copy in copies:
        copy.wait()
    me = my_index()
    for head in range(LINE):
        at = slice(head * HEAD, head * HEAD + HEAD)
        both = jnp.concatenate([teacher_ref[:, at], student_ref[:, at]], axis=1)
        for turn, out_ref in enumerate(out_refs):

            @pl.when((me >> 3) == (head ^ MET_X[turn]))
            def _():
                out_ref[...] = both


def plan_kernel(far, table_hbm_ref, plan_ref, table_ref, sem_ref):
    copy = pltpu.make_async_copy(table_hbm_ref, table_ref, sem_ref)
    copy.start()
    me = my_index()
    core = me & 1
    side = core ^ far
    copy.wait()

    def listed(row, first, prefix):
        inside = [(table_ref[row, 2 * k + side] >= 0).astype(jnp.int32) for k in range(SIDE)]
        at = first
        for k in range(SIDE):
            plan_ref[at] = prefix + k
            at = at + inside[k]
        return at

    def filled(at, count, word):
        for k in range(count):
            plan_ref[at + k] = word

    end = lax.fori_loop(
        0, SIDE, lambda i, at: listed(2 * i + core, at, i * BLOCKS), jnp.int32(PAIRS_AT)
    )
    filled(end, UNROLL, SIDE * BLOCKS)
    plan_ref[0] = end - PAIRS_AT

    def own(b, at):
        end = listed(me ^ (b << 3), at, b * BLOCKS)
        filled(end, CHUNK - 1, b * BLOCKS + SIDE)
        return OWN_AT + (end - OWN_AT + CHUNK - 1) // CHUNK * CHUNK

    end = lax.fori_loop(0, LINE, own, jnp.int32(OWN_AT))
    filled(end, CHUNK * OWN_UNROLL, LINE * BLOCKS + SIDE)
    plan_ref[1] = (end - OWN_AT) // CHUNK


def spread(in_ref, rows_ref, wide_ref):
    me = my_index()
    zero = jnp.zeros((HEAD, ROWS), jnp.bfloat16)
    for slot in range(SIDE):
        at = (me >> 1) ^ ((MET_X[slot & 3] << 2) | MET_Y[slot >> 2])
        tile = in_ref[slot]
        rows_ref[at] = tile
        flipped = tile.astype(jnp.float32).T.astype(jnp.bfloat16)
        wide_ref[at, :, :ROWS] = jnp.concatenate([flipped[:HEAD], zero], axis=0)
        wide_ref[at, :, ROWS:] = jnp.concatenate([zero, flipped[HEAD:]], axis=0)
    rows_ref[SIDE] = jnp.zeros((ROWS, ROWS), jnp.bfloat16)
    wide_ref[SIDE] = jnp.zeros((ROWS, 2 * ROWS), jnp.bfloat16)


def scores(left, right):
    return jnp.dot(left, right, preferred_element_type=jnp.float32)


def folded(a):
    return jnp.sum(a.reshape(ROWS // 8, 8, ROWS), axis=0)


def totals(exps, raw):
    teacher, student = exps[:, :ROWS], exps[:, ROWS:]
    gap = teacher * (raw[:, :ROWS] - raw[:, ROWS:])
    return folded(teacher), folded(student), folded(gap)


def add_totals(plan_ref, rows_ref, wide_ref, acc_ref):
    pairs = plan_ref[0]

    def turn(first, count):
        done = []
        for k in range(count):
            word = plan_ref[first + k]
            row, column = word >> 5, word & (BLOCKS - 1)
            raw = scores(rows_ref[column], wide_ref[row])
            done.append((row, totals(jnp.exp2(raw * (SCALE * LOG2E)), raw)))
        for row, parts in done:
            for k, part in enumerate(parts):
                acc_ref[row, k] += part
        return 0

    long = pairs // (2 * UNROLL)
    lax.fori_loop(0, long, lambda n, c: turn(PAIRS_AT + n * 2 * UNROLL, 2 * UNROLL), 0)
    rest = pairs - long * 2 * UNROLL
    lax.fori_loop(
        0,
        (rest + UNROLL - 1) // UNROLL,
        lambda n, c: turn(PAIRS_AT + (2 * long + n) * UNROLL, UNROLL),
        0,
    )


def fetched(plan_in_ref, plan_ref, sem_ref):
    copy = pltpu.make_async_copy(plan_in_ref, plan_ref, sem_ref)
    copy.start()
    return copy


def near_kernel(plan_in_ref, half_ref, rows_ref, wide_ref, acc_ref, plan_ref, sem_ref):
    copy = fetched(plan_in_ref, plan_ref, sem_ref)
    spread(half_ref, rows_ref, wide_ref)
    acc_ref[...] = jnp.zeros_like(acc_ref)
    copy.wait()
    add_totals(plan_ref, rows_ref, wide_ref, acc_ref)


def far_kernel(
    near_plan_in_ref,
    plan_in_ref,
    other_ref,
    near_rows_ref,
    near_wide_ref,
    near_acc_ref,
    rows_ref,
    wide_ref,
    sent_ref,
    acc_ref,
    top_ref,
    near_plan_ref,
    near_sem_ref,
    plan_ref,
    sem_ref,
):
    near_copy = fetched(near_plan_in_ref, near_plan_ref, near_sem_ref)
    copy = fetched(plan_in_ref, plan_ref, sem_ref)
    spread(other_ref, rows_ref, wide_ref)
    acc_ref[...] = near_acc_ref[...]
    near_copy.wait()
    copy.wait()
    add_totals(plan_ref, rows_ref, near_wide_ref, acc_ref)

    def row_sums(k):
        return jnp.sum(acc_ref[:SIDE, k], axis=1)

    def finished(teacher_log, student_log, gap_mean, flag):
        sent_ref[:SIDE] = teacher_log
        sent_ref[SIDE : 2 * SIDE] = student_log
        per_row = gap_mean * SCALE - teacher_log + student_log
        row = lax.broadcasted_iota(jnp.int32, (8, ROWS), 0)
        sent_ref[DIV_AT:] = jnp.where(
            row == 0, jnp.sum(per_row, axis=0, keepdims=True), jnp.where(row == 1, flag, 0.0)
        )

    teacher_sum, student_sum, gap_sum = row_sums(0), row_sums(1), row_sums(2)
    fine = (
        (teacher_sum < SUM_LIMIT) & (student_sum < SUM_LIMIT) & (jnp.abs(gap_sum) < SUM_LIMIT)
    )
    safe = jnp.min(fine.astype(jnp.float32)) > 0.5

    @pl.when(safe)
    def _():
        finished(jnp.log(teacher_sum), jnp.log(student_sum), gap_sum / teacher_sum, 0.0)

    @pl.when(jnp.logical_not(safe))
    def _():
        top_ref[...] = jnp.full_like(top_ref, FLOOR)
        acc_ref[...] = jnp.zeros_like(acc_ref)
        lists = ((near_plan_ref, near_rows_ref), (plan_ref, rows_ref))

        def each_pair(act):
            for list_ref, left_ref in lists:

                def turn(n, carry):
                    word = list_ref[PAIRS_AT + n]
                    row, column = word >> 5, word & (BLOCKS - 1)
                    act(row, scores(left_ref[column], near_wide_ref[row]))
                    return carry

                lax.fori_loop(0, list_ref[0], turn, 0)

        def raise_top(row, raw):
            top = jnp.max(raw, axis=0, keepdims=True) * SCALE
            for k in range(2):
                at = (k, pl.ds(row, 1), slice(None))
                top_ref[at] = jnp.maximum(top_ref[at], top[:, k * ROWS : (k + 1) * ROWS])

        def add_shifted(row, raw):
            top = jnp.concatenate([top_ref[k, pl.ds(row, 1), :] for k in range(2)], axis=1)
            for k, part in enumerate(totals(jnp.exp(raw * SCALE - top), raw)):
                acc_ref[row, k] += part

        each_pair(raise_top)
        each_pair(add_shifted)
        teacher_sum, student_sum, gap_sum = row_sums(0), row_sums(1), row_sums(2)
        finished(
            top_ref[0] + jnp.log(teacher_sum),
            top_ref[1] + jnp.log(student_sum),
            gap_sum / teacher_sum,
            1.0,
        )


def along_rows(row):
    return jnp.broadcast_to(row, (ROWS, ROWS)).T


def own_at(b):
    return (my_index() >> 1) ^ ((b & 3) << 2)


def is_safe(sent_ref):
    return jnp.max(sent_ref[FLAG_AT : FLAG_AT + 1]) < 0.5


def fill_columns(col_ref, value, near_sent_ref):
    for b in range(LINE):
        for k in range(2):
            row = near_sent_ref[pl.ds(own_at(b) + k * SIDE, 1), :]
            col_ref[b, k] = along_rows(value(row))


def safe_gradient(
    plan_ref, near_rows_ref, rows_ref, wide_ref, sent_ref, inv_ref, col_ref, grad_ref, copy
):
    inv_ref[...] = jnp.zeros_like(inv_ref)
    for k in range(2):
        inv_ref[k, :SIDE] = jnp.exp(-sent_ref[k * SIDE : (k + 1) * SIDE])
    copy.wait()
    chunks = plan_ref[1]

    def turn(group, carry):
        words = [
            [plan_ref[OWN_AT + (group * OWN_UNROLL + k) * CHUNK + n] for n in range(CHUNK)]
            for k in range(OWN_UNROLL)
        ]
        owns = [chunk[0] >> 5 for chunk in words]
        columns = [[w & (BLOCKS - 1) for w in chunk] for chunk in words]
        raws = [
            scores(
                near_rows_ref[own_at(b)], jnp.concatenate([wide_ref[c] for c in chunk], axis=1)
            )
            for b, chunk in zip(owns, columns)
        ]
        symmetric = []
        for b, chunk, raw in zip(owns, columns, raws):
            parts = []
            for n, c in enumerate(chunk):
                exps = jnp.exp2(raw[:, 2 * ROWS * n : 2 * ROWS * (n + 1)] * (SCALE * LOG2E))
                teacher_inv = col_ref[b, 0] + inv_ref[0, pl.ds(c, 1), :]
                student_inv = col_ref[b, 1] + inv_ref[1, pl.ds(c, 1), :]
                gap = exps[:, ROWS:] * student_inv - exps[:, :ROWS] * teacher_inv
                parts.append(gap.astype(jnp.bfloat16))
            symmetric.append(jnp.concatenate(parts, axis=1))
        done = [
            (b, scores(sym, jnp.concatenate([rows_ref[c] for c in chunk], axis=0)))
            for b, chunk, sym in zip(owns, columns, symmetric)
        ]
        for b, part in done:
            grad_ref[b] += part
        return carry

    lax.fori_loop(0, (chunks + OWN_UNROLL - 1) // OWN_UNROLL, turn, 0)


def shifted_gradient(
    plan_ref, near_rows_ref, rows_ref, wide_ref, sent_ref, inv_ref, col_ref, grad_ref, copy
):
    inv_ref[...] = jnp.zeros_like(inv_ref)
    for k in range(2):
        inv_ref[k, :SIDE] = sent_ref[k * SIDE : (k + 1) * SIDE]
    copy.wait()
    chunks = plan_ref[1]

    def turn(n, carry):
        word = plan_ref[OWN_AT + n]
        b, c = word >> 5, word & (BLOCKS - 1)

        @pl.when(c < SIDE)
        def _():
            raw = scores(near_rows_ref[own_at(b)], wide_ref[c]) * SCALE
            teacher, student = raw[:, :ROWS], raw[:, ROWS:]
            row_gap = jnp.exp(student - col_ref[b, 1]) - jnp.exp(teacher - col_ref[b, 0])
            column_gap = jnp.exp(student - inv_ref[1, pl.ds(c, 1), :]) - jnp.exp(
                teacher - inv_ref[0, pl.ds(c, 1), :]
            )
            grad_ref[b] += scores((row_gap + column_gap).astype(jnp.bfloat16), rows_ref[c])

        return carry

    lax.fori_loop(0, chunks * CHUNK, turn, 0)


def near_grad_kernel(
    plan_in_ref, rows_ref, wide_ref, sent_ref, grad_ref, col_ref, inv_ref, plan_ref, sem_ref
):
    copy = fetched(plan_in_ref, plan_ref, sem_ref)
    grad_ref[...] = jnp.zeros_like(grad_ref)
    col_ref[LINE] = jnp.zeros((2, ROWS, ROWS), jnp.float32)
    rest = (plan_ref, rows_ref, rows_ref, wide_ref, sent_ref)
    safe = is_safe(sent_ref)

    @pl.when(safe)
    def _():
        fill_columns(col_ref, lambda row: jnp.exp(-row), sent_ref)
        safe_gradient(*rest, inv_ref, col_ref, grad_ref, copy)

    @pl.when(jnp.logical_not(safe))
    def _():
        fill_columns(col_ref, lambda row: row, sent_ref)
        shifted_gradient(*rest, inv_ref, col_ref, grad_ref, copy)


def far_grad_kernel(
    plan_in_ref,
    near_rows_ref,
    rows_ref,
    wide_ref,
    near_sent_ref,
    sent_ref,
    near_grad_ref,
    near_col_ref,
    *refs,
):
    out_refs, (inv_ref, grad_ref, col_ref, plan_ref, sem_ref) = refs[:LINE], refs[LINE:]
    copy = fetched(plan_in_ref, plan_ref, sem_ref)
    grad_ref[...] = near_grad_ref[...]
    rest = (plan_ref, near_rows_ref, rows_ref, wide_ref, sent_ref)
    safe = is_safe(sent_ref) & is_safe(near_sent_ref)

    @pl.when(safe)
    def _():
        safe_gradient(*rest, inv_ref, near_col_ref, grad_ref, copy)

    @pl.when(jnp.logical_not(safe))
    def _():
        col_ref[LINE] = jnp.zeros((2, ROWS, ROWS), jnp.float32)
        fill_columns(col_ref, lambda row: row, near_sent_ref)
        shifted_gradient(*rest, inv_ref, col_ref, grad_ref, copy)

    div = jnp.sum(
        near_sent_ref[DIV_AT : DIV_AT + 1] + sent_ref[DIV_AT : DIV_AT + 1], axis=1, keepdims=True
    ) * (1.0 / (BLOCKS * ROWS))
    high = div.astype(jnp.bfloat16).astype(jnp.float32)
    middle = (div - high).astype(jnp.bfloat16).astype(jnp.float32)
    low = div - high - middle
    lane = lax.broadcasted_iota(jnp.int32, (16, ROWS), 1)
    tail = jnp.where(lane == 0, high, jnp.where(lane == 1, middle, jnp.where(lane == 2, low, 0.0)))
    left = lax.broadcasted_iota(jnp.int32, (HALF, ROWS), 1) < HEAD
    for k, out_ref in enumerate(out_refs):
        total = grad_ref[MET_BACK[k]] * WEIGHT
        packed = jnp.where(left, pltpu.roll(total[:HALF], HEAD, 1), total[HALF:])
        out_ref[:HALF] = packed.astype(jnp.bfloat16)
        out_ref[HALF:] = tail.astype(jnp.bfloat16)


def assemble_kernel(*refs):
    in_refs, (grad_ref, div_ref) = refs[:LINE], refs[LINE:]
    x = my_index() >> 3
    for case in range(LINE):

        @pl.when(x == case)
        def _():
            for head in range(LINE):
                from_ref = in_refs[MET_BACK.index(head ^ case)]
                at = slice(head * HEAD, head * HEAD + HEAD)
                grad_ref[:HALF, at] = from_ref[:HALF, :HEAD]
                grad_ref[HALF:, at] = from_ref[:HALF, HEAD:]
                div_ref[head] = jnp.sum(from_ref[HALF:].astype(jnp.float32)[:1])


def shape(*dims, dtype=jnp.bfloat16):
    return jax.ShapeDtypeStruct(dims, dtype)


def call(kernel, name, out_shape, in_specs, out_specs, scratch=(), limit=12 << 20):
    return pl.pallas_call(
        kernel,
        out_shape=out_shape,
        in_specs=in_specs,
        out_specs=out_specs,
        scratch_shapes=list(scratch),
        compiler_params=pltpu.CompilerParams(vmem_limit_bytes=limit),
        name=name,
    )


F32 = jnp.float32
BLOCK_SET = shape(SIDE + 1, ROWS, ROWS)
WIDE_SET = shape(SIDE + 1, ROWS, 2 * ROWS)
ACC = (SIDE + 1, 3, 8, ROWS)
GRAD = (LINE + 1, ROWS, ROWS)
COL = (LINE + 1, 2, ROWS, ROWS)
INV = pltpu.VMEM((2, SIDE + 8, ROWS), F32)
PLAN = [pltpu.SMEM((PLAN_LEN,), jnp.int32), pltpu.SemaphoreType.DMA]


def plan_call(owner_table, far):
    return call(
        functools.partial(plan_kernel, far),
        ("list_near_pairs", "list_far_pairs")[far],
        shape(PLAN_LEN, dtype=jnp.int32),
        [pl.BlockSpec(memory_space=pltpu.HBM)],
        SMEM,
        [pltpu.SMEM((BLOCKS, BLOCKS), jnp.int32), pltpu.SemaphoreType.DMA],
        limit=1 << 20,
    )(pltpu.with_memory_space_constraint(owner_table, pltpu.HBM))


def near_call(plan, half):
    return call(
        near_kernel,
        "near_sums",
        [BLOCK_SET, WIDE_SET, shape(*ACC, dtype=F32)],
        [VMEM] * 2,
        [VMEM] * 3,
        PLAN,
    )(plan, half)


def far_call(near_plan, plan, other, near_rows, near_wide, near_acc):
    return call(
        far_kernel,
        "far_sums",
        [BLOCK_SET, WIDE_SET, shape(SENT, ROWS, dtype=F32)],
        [VMEM] * 6,
        [VMEM] * 3,
        [pltpu.VMEM(ACC, F32), pltpu.VMEM((2, SIDE, ROWS), F32), *PLAN, *PLAN],
    )(near_plan, plan, other, near_rows, near_wide, near_acc)


def near_grad_call(plan, near_rows, near_wide, near_sent):
    return call(
        near_grad_kernel,
        "near_gradient",
        [shape(*GRAD, dtype=F32), shape(*COL, dtype=F32)],
        [VMEM] * 4,
        [VMEM] * 2,
        [INV, *PLAN],
    )(plan, near_rows, near_wide, near_sent)


def far_grad_call(*arrays):
    return call(
        far_grad_kernel,
        "far_gradient",
        [shape(HALF + 16, ROWS)] * LINE,
        [VMEM] * 8,
        [VMEM] * LINE,
        [INV, pltpu.VMEM(GRAD, F32), pltpu.VMEM(COL, F32), *PLAN],
    )(*arrays)


def per_device(teacher_q, student_q, owner_table):
    slices = call(
        slice_kernel,
        "slice_heads",
        [shape(ROWS, ROWS)] * LINE,
        [pl.BlockSpec(memory_space=pltpu.HBM)] * 2,
        [VMEM] * LINE,
        [pltpu.VMEM(teacher_q.shape, jnp.bfloat16)] * 2 + [pltpu.SemaphoreType.DMA((2,))],
        limit=2 << 20,
    )(*[pltpu.with_memory_space_constraint(a, pltpu.HBM) for a in (teacher_q, student_q)])
    near_plan, far_plan = plan_call(owner_table, 0), plan_call(owner_table, 1)
    line = jnp.stack([slices[0]] + [exchanged(slices[b], MET_X[b], 3) for b in (1, 2, 3)])
    line, near_plan = lax.optimization_barrier((line, near_plan))
    half = jnp.concatenate([line] + [exchanged(line, MET_Y[a], 1) for a in (1, 2, 3)])
    half, far_plan = lax.optimization_barrier((half, far_plan))
    other = swapped(half)
    near_rows, near_wide, near_acc = near_call(near_plan, half)
    far_rows, far_wide, near_sent = far_call(
        near_plan, far_plan, other, near_rows, near_wide, near_acc
    )
    far_sent = swapped(near_sent)
    near_grad, near_col = near_grad_call(near_plan, near_rows, near_wide, near_sent)
    grads = far_grad_call(
        far_plan, near_rows, far_rows, far_wide, near_sent, far_sent, near_grad, near_col
    )
    back = [grads[0]] + [exchanged(grads[b], MET_BACK[b], 3) for b in (1, 2, 3)]
    return call(
        assemble_kernel,
        "assemble",
        [shape(*teacher_q.shape), shape(LINE, dtype=F32)],
        [VMEM] * LINE,
        [VMEM, SMEM],
        limit=2 << 20,
    )(*back)


def solution(mesh):
    placed = (P("tok", "head"), P("tok", "head"), P())
    return jax.shard_map(
        lambda *arrays: tuple(per_device(*arrays)),
        mesh=mesh,
        in_specs=placed,
        out_specs=(P("tok", "head"), P("head")),
        check_vma=False,
    )
```

```python
import functools

import jax
import jax.numpy as jnp
from jax import lax
from jax.experimental import pallas as pl
from jax.experimental.pallas import tpu as pltpu
from jax.sharding import PartitionSpec as P

HEAD = 64
ROWS = 128
HALF = ROWS // 2
BLOCKS = 32
SIDE = BLOCKS // 2
LINE = 4
LOG2E = 1.4426950408889634
SCALE = HEAD**-0.5
WEIGHT = 32.0 * SCALE
SUM_LIMIT = 2.0**100
FLOOR = -1e30
UNROLL = 16
CHUNK = 4
OWN_UNROLL = 8
OWN_FEW = 6
PAIRS_AT = 8
OWN_AT = PAIRS_AT + SIDE * SIDE + UNROLL
PLAN_LEN = OWN_AT + LINE * SIDE + CHUNK * OWN_UNROLL + CHUNK
DIV_AT = 2 * SIDE
FLAG_AT = DIV_AT + 1
SENT = DIV_AT + 8
VMEM = pl.BlockSpec(memory_space=pltpu.VMEM)
SMEM = pl.BlockSpec(memory_space=pltpu.SMEM)


def my_index():
    return lax.axis_index("tok")


MET_X = (0, 3, 2, 1)
MET_Y = (0, 1, 3, 2)
MET_BACK = (0, 2, 3, 1)


def exchanged(array, code, shift):
    return lax.ppermute(array, "tok", [(i, i ^ (code << shift)) for i in range(BLOCKS)])


def swapped(array):
    return lax.ppermute(array, "tok", [(i, i ^ 1) for i in range(BLOCKS)])


def slice_kernel(teacher_hbm_ref, student_hbm_ref, *refs):
    out_refs, (teacher_ref, student_ref, sem_ref) = refs[:LINE], refs[LINE:]
    copies = [
        pltpu.make_async_copy(teacher_hbm_ref, teacher_ref, sem_ref.at[0]),
        pltpu.make_async_copy(student_hbm_ref, student_ref, sem_ref.at[1]),
    ]
    for copy in copies:
        copy.start()
    for copy in copies:
        copy.wait()
    me = my_index()
    for head in range(LINE):
        at = slice(head * HEAD, head * HEAD + HEAD)
        both = jnp.concatenate([teacher_ref[:, at], student_ref[:, at]], axis=1)
        for turn, out_ref in enumerate(out_refs):

            @pl.when((me >> 3) == (head ^ MET_X[turn]))
            def _():
                out_ref[...] = both


def plan_kernel(far, table_hbm_ref, plan_ref, table_ref, sem_ref):
    copy = pltpu.make_async_copy(table_hbm_ref, table_ref, sem_ref)
    copy.start()
    me = my_index()
    core = me & 1
    side = core ^ far
    copy.wait()

    def listed(row, first, prefix):
        inside = [(table_ref[row, 2 * k + side] >= 0).astype(jnp.int32) for k in range(SIDE)]
        at = first
        for k in range(SIDE):
            plan_ref[at] = prefix + k
            at = at + inside[k]
        return at

    def filled(at, count, word):
        for k in range(count):
            plan_ref[at + k] = word

    end = lax.fori_loop(
        0, SIDE, lambda i, at: listed(2 * i + core, at, i * BLOCKS), jnp.int32(PAIRS_AT)
    )
    filled(end, UNROLL, SIDE * BLOCKS)
    plan_ref[0] = end - PAIRS_AT

    def own(b, at):
        end = listed(me ^ (b << 3), at, b * BLOCKS)
        filled(end, CHUNK - 1, b * BLOCKS + SIDE)
        return OWN_AT + (end - OWN_AT + CHUNK - 1) // CHUNK * CHUNK

    end = lax.fori_loop(0, LINE, own, jnp.int32(OWN_AT))
    filled(end, CHUNK * OWN_UNROLL, LINE * BLOCKS + SIDE)
    plan_ref[1] = (end - OWN_AT) // CHUNK


def spread(in_ref, rows_ref, wide_ref):
    me = my_index()
    zero = jnp.zeros((HEAD, ROWS), jnp.bfloat16)
    for slot in range(SIDE):
        at = (me >> 1) ^ ((MET_X[slot & 3] << 2) | MET_Y[slot >> 2])
        tile = in_ref[slot]
        rows_ref[at] = tile
        flipped = tile.astype(jnp.float32).T.astype(jnp.bfloat16)
        wide_ref[at, :, :ROWS] = jnp.concatenate([flipped[:HEAD], zero], axis=0)
        wide_ref[at, :, ROWS:] = jnp.concatenate([zero, flipped[HEAD:]], axis=0)
    rows_ref[SIDE] = jnp.zeros((ROWS, ROWS), jnp.bfloat16)
    wide_ref[SIDE] = jnp.zeros((ROWS, 2 * ROWS), jnp.bfloat16)


def scores(left, right):
    return jnp.dot(left, right, preferred_element_type=jnp.float32)


def folded(a):
    return jnp.sum(a.reshape(ROWS // 8, 8, ROWS), axis=0)


def totals(exps, raw):
    teacher, student = exps[:, :ROWS], exps[:, ROWS:]
    gap = teacher * (raw[:, :ROWS] - raw[:, ROWS:])
    return folded(teacher), folded(student), folded(gap)


def add_totals(plan_ref, rows_ref, wide_ref, acc_ref):
    pairs = plan_ref[0]

    def turn(first, count):
        done = []
        for k in range(count):
            word = plan_ref[first + k]
            row, column = word >> 5, word & (BLOCKS - 1)
            raw = scores(rows_ref[column], wide_ref[row])
            done.append((row, totals(jnp.exp2(raw * (SCALE * LOG2E)), raw)))
        for row, parts in done:
            for k, part in enumerate(parts):
                acc_ref[row, k] += part
        return 0

    long = pairs // (2 * UNROLL)
    lax.fori_loop(0, long, lambda n, c: turn(PAIRS_AT + n * 2 * UNROLL, 2 * UNROLL), 0)
    rest = pairs - long * 2 * UNROLL
    lax.fori_loop(
        0,
        (rest + UNROLL - 1) // UNROLL,
        lambda n, c: turn(PAIRS_AT + (2 * long + n) * UNROLL, UNROLL),
        0,
    )


def fetched(plan_in_ref, plan_ref, sem_ref):
    copy = pltpu.make_async_copy(plan_in_ref, plan_ref, sem_ref)
    copy.start()
    return copy


def near_kernel(plan_in_ref, half_ref, rows_ref, wide_ref, acc_ref, plan_ref, sem_ref):
    copy = fetched(plan_in_ref, plan_ref, sem_ref)
    spread(half_ref, rows_ref, wide_ref)
    acc_ref[...] = jnp.zeros_like(acc_ref)
    copy.wait()
    add_totals(plan_ref, rows_ref, wide_ref, acc_ref)


def far_kernel(
    near_plan_in_ref,
    plan_in_ref,
    other_ref,
    near_rows_ref,
    near_wide_ref,
    near_acc_ref,
    rows_ref,
    wide_ref,
    sent_ref,
    acc_ref,
    top_ref,
    near_plan_ref,
    near_sem_ref,
    plan_ref,
    sem_ref,
):
    near_copy = fetched(near_plan_in_ref, near_plan_ref, near_sem_ref)
    copy = fetched(plan_in_ref, plan_ref, sem_ref)
    spread(other_ref, rows_ref, wide_ref)
    acc_ref[...] = near_acc_ref[...]
    near_copy.wait()
    copy.wait()
    add_totals(plan_ref, rows_ref, near_wide_ref, acc_ref)

    def row_sums(k):
        return jnp.sum(acc_ref[:SIDE, k], axis=1)

    def finished(teacher_log, student_log, gap_mean, flag):
        sent_ref[:SIDE] = teacher_log
        sent_ref[SIDE : 2 * SIDE] = student_log
        per_row = gap_mean * SCALE - teacher_log + student_log
        row = lax.broadcasted_iota(jnp.int32, (8, ROWS), 0)
        sent_ref[DIV_AT:] = jnp.where(
            row == 0, jnp.sum(per_row, axis=0, keepdims=True), jnp.where(row == 1, flag, 0.0)
        )

    teacher_sum, student_sum, gap_sum = row_sums(0), row_sums(1), row_sums(2)
    fine = (
        (teacher_sum < SUM_LIMIT) & (student_sum < SUM_LIMIT) & (jnp.abs(gap_sum) < SUM_LIMIT)
    )
    safe = jnp.min(fine.astype(jnp.float32)) > 0.5

    @pl.when(safe)
    def _():
        finished(jnp.log(teacher_sum), jnp.log(student_sum), gap_sum / teacher_sum, 0.0)

    @pl.when(jnp.logical_not(safe))
    def _():
        top_ref[...] = jnp.full_like(top_ref, FLOOR)
        acc_ref[...] = jnp.zeros_like(acc_ref)
        lists = ((near_plan_ref, near_rows_ref), (plan_ref, rows_ref))

        def each_pair(act):
            for list_ref, left_ref in lists:

                def turn(n, carry):
                    word = list_ref[PAIRS_AT + n]
                    row, column = word >> 5, word & (BLOCKS - 1)
                    act(row, scores(left_ref[column], near_wide_ref[row]))
                    return carry

                lax.fori_loop(0, list_ref[0], turn, 0)

        def raise_top(row, raw):
            top = jnp.max(raw, axis=0, keepdims=True) * SCALE
            for k in range(2):
                at = (k, pl.ds(row, 1), slice(None))
                top_ref[at] = jnp.maximum(top_ref[at], top[:, k * ROWS : (k + 1) * ROWS])

        def add_shifted(row, raw):
            top = jnp.concatenate([top_ref[k, pl.ds(row, 1), :] for k in range(2)], axis=1)
            for k, part in enumerate(totals(jnp.exp(raw * SCALE - top), raw)):
                acc_ref[row, k] += part

        each_pair(raise_top)
        each_pair(add_shifted)
        teacher_sum, student_sum, gap_sum = row_sums(0), row_sums(1), row_sums(2)
        finished(
            top_ref[0] + jnp.log(teacher_sum),
            top_ref[1] + jnp.log(student_sum),
            gap_sum / teacher_sum,
            1.0,
        )


def along_rows(row):
    return jnp.broadcast_to(row, (ROWS, ROWS)).T


def own_at(b):
    return (my_index() >> 1) ^ ((b & 3) << 2)


def is_safe(sent_ref):
    return jnp.max(sent_ref[FLAG_AT : FLAG_AT + 1]) < 0.5


def fill_columns(col_ref, value, near_sent_ref):
    for b in range(LINE):
        for k in range(2):
            row = near_sent_ref[pl.ds(own_at(b) + k * SIDE, 1), :]
            col_ref[b, k] = along_rows(value(row))


def safe_gradient(
    plan_ref, near_rows_ref, rows_ref, wide_ref, sent_ref, inv_ref, col_ref, grad_ref, copy
):
    inv_ref[...] = jnp.zeros_like(inv_ref)
    for k in range(2):
        inv_ref[k, :SIDE] = jnp.exp(-sent_ref[k * SIDE : (k + 1) * SIDE])
    copy.wait()
    chunks = plan_ref[1]

    def turn(at, count):
        words = [
            [plan_ref[at + k * CHUNK + n] for n in range(CHUNK)]
            for k in range(count)
        ]
        owns = [chunk[0] >> 5 for chunk in words]
        columns = [[w & (BLOCKS - 1) for w in chunk] for chunk in words]
        raws = [
            scores(
                near_rows_ref[own_at(b)], jnp.concatenate([wide_ref[c] for c in chunk], axis=1)
            )
            for b, chunk in zip(owns, columns)
        ]
        symmetric = []
        for b, chunk, raw in zip(owns, columns, raws):
            parts = []
            for n, c in enumerate(chunk):
                exps = jnp.exp2(raw[:, 2 * ROWS * n : 2 * ROWS * (n + 1)] * (SCALE * LOG2E))
                teacher_inv = col_ref[b, 0] + inv_ref[0, pl.ds(c, 1), :]
                student_inv = col_ref[b, 1] + inv_ref[1, pl.ds(c, 1), :]
                gap = exps[:, ROWS:] * student_inv - exps[:, :ROWS] * teacher_inv
                parts.append(gap.astype(jnp.bfloat16))
            symmetric.append(jnp.concatenate(parts, axis=1))
        done = [
            (b, scores(sym, jnp.concatenate([rows_ref[c] for c in chunk], axis=0)))
            for b, chunk, sym in zip(owns, columns, symmetric)
        ]
        for b, part in done:
            grad_ref[b] += part
        return 0

    few = chunks <= OWN_FEW
    lax.fori_loop(0, few.astype(jnp.int32), lambda n, c: turn(OWN_AT, OWN_FEW), 0)
    lax.fori_loop(
        0,
        jnp.where(few, 0, (chunks + OWN_UNROLL - 1) // OWN_UNROLL),
        lambda n, c: turn(OWN_AT + n * (OWN_UNROLL * CHUNK), OWN_UNROLL),
        0,
    )


def shifted_gradient(
    plan_ref, near_rows_ref, rows_ref, wide_ref, sent_ref, inv_ref, col_ref, grad_ref, copy
):
    inv_ref[...] = jnp.zeros_like(inv_ref)
    for k in range(2):
        inv_ref[k, :SIDE] = sent_ref[k * SIDE : (k + 1) * SIDE]
    copy.wait()
    chunks = plan_ref[1]

    def turn(n, carry):
        word = plan_ref[OWN_AT + n]
        b, c = word >> 5, word & (BLOCKS - 1)

        @pl.when(c < SIDE)
        def _():
            raw = scores(near_rows_ref[own_at(b)], wide_ref[c]) * SCALE
            teacher, student = raw[:, :ROWS], raw[:, ROWS:]
            row_gap = jnp.exp(student - col_ref[b, 1]) - jnp.exp(teacher - col_ref[b, 0])
            column_gap = jnp.exp(student - inv_ref[1, pl.ds(c, 1), :]) - jnp.exp(
                teacher - inv_ref[0, pl.ds(c, 1), :]
            )
            grad_ref[b] += scores((row_gap + column_gap).astype(jnp.bfloat16), rows_ref[c])

        return carry

    lax.fori_loop(0, chunks * CHUNK, turn, 0)


def near_grad_kernel(
    plan_in_ref, rows_ref, wide_ref, sent_ref, grad_ref, col_ref, inv_ref, plan_ref, sem_ref
):
    copy = fetched(plan_in_ref, plan_ref, sem_ref)
    grad_ref[...] = jnp.zeros_like(grad_ref)
    col_ref[LINE] = jnp.zeros((2, ROWS, ROWS), jnp.float32)
    rest = (plan_ref, rows_ref, rows_ref, wide_ref, sent_ref)
    safe = is_safe(sent_ref)

    @pl.when(safe)
    def _():
        fill_columns(col_ref, lambda row: jnp.exp(-row), sent_ref)
        safe_gradient(*rest, inv_ref, col_ref, grad_ref, copy)

    @pl.when(jnp.logical_not(safe))
    def _():
        fill_columns(col_ref, lambda row: row, sent_ref)
        shifted_gradient(*rest, inv_ref, col_ref, grad_ref, copy)


def far_grad_kernel(
    plan_in_ref,
    near_rows_ref,
    rows_ref,
    wide_ref,
    near_sent_ref,
    sent_ref,
    near_grad_ref,
    near_col_ref,
    *refs,
):
    out_refs, (inv_ref, grad_ref, col_ref, plan_ref, sem_ref) = refs[:LINE], refs[LINE:]
    copy = fetched(plan_in_ref, plan_ref, sem_ref)
    grad_ref[...] = near_grad_ref[...]
    rest = (plan_ref, near_rows_ref, rows_ref, wide_ref, sent_ref)
    safe = is_safe(sent_ref) & is_safe(near_sent_ref)

    @pl.when(safe)
    def _():
        safe_gradient(*rest, inv_ref, near_col_ref, grad_ref, copy)

    @pl.when(jnp.logical_not(safe))
    def _():
        col_ref[LINE] = jnp.zeros((2, ROWS, ROWS), jnp.float32)
        fill_columns(col_ref, lambda row: row, near_sent_ref)
        shifted_gradient(*rest, inv_ref, col_ref, grad_ref, copy)

    div = jnp.sum(
        near_sent_ref[DIV_AT : DIV_AT + 1] + sent_ref[DIV_AT : DIV_AT + 1], axis=1, keepdims=True
    ) * (1.0 / (BLOCKS * ROWS))
    high = div.astype(jnp.bfloat16).astype(jnp.float32)
    middle = (div - high).astype(jnp.bfloat16).astype(jnp.float32)
    low = div - high - middle
    lane = lax.broadcasted_iota(jnp.int32, (16, ROWS), 1)
    tail = jnp.where(lane == 0, high, jnp.where(lane == 1, middle, jnp.where(lane == 2, low, 0.0)))
    left = lax.broadcasted_iota(jnp.int32, (HALF, ROWS), 1) < HEAD
    for k, out_ref in enumerate(out_refs):
        total = grad_ref[MET_BACK[k]] * WEIGHT
        packed = jnp.where(left, pltpu.roll(total[:HALF], HEAD, 1), total[HALF:])
        out_ref[:HALF] = packed.astype(jnp.bfloat16)
        out_ref[HALF:] = tail.astype(jnp.bfloat16)


def assemble_kernel(*refs):
    in_refs, (grad_ref, div_ref) = refs[:LINE], refs[LINE:]
    x = my_index() >> 3
    for case in range(LINE):

        @pl.when(x == case)
        def _():
            for head in range(LINE):
                from_ref = in_refs[MET_BACK.index(head ^ case)]
                at = slice(head * HEAD, head * HEAD + HEAD)
                grad_ref[:HALF, at] = from_ref[:HALF, :HEAD]
                grad_ref[HALF:, at] = from_ref[:HALF, HEAD:]
                div_ref[head] = jnp.sum(from_ref[HALF:].astype(jnp.float32)[:1])


def shape(*dims, dtype=jnp.bfloat16):
    return jax.ShapeDtypeStruct(dims, dtype)


def call(kernel, name, out_shape, in_specs, out_specs, scratch=(), limit=12 << 20):
    return pl.pallas_call(
        kernel,
        out_shape=out_shape,
        in_specs=in_specs,
        out_specs=out_specs,
        scratch_shapes=list(scratch),
        compiler_params=pltpu.CompilerParams(vmem_limit_bytes=limit),
        name=name,
    )


F32 = jnp.float32
BLOCK_SET = shape(SIDE + 1, ROWS, ROWS)
WIDE_SET = shape(SIDE + 1, ROWS, 2 * ROWS)
ACC = (SIDE + 1, 3, 8, ROWS)
GRAD = (LINE + 1, ROWS, ROWS)
COL = (LINE + 1, 2, ROWS, ROWS)
INV = pltpu.VMEM((2, SIDE + 8, ROWS), F32)
PLAN = [pltpu.SMEM((PLAN_LEN,), jnp.int32), pltpu.SemaphoreType.DMA]


def plan_call(owner_table, far):
    return call(
        functools.partial(plan_kernel, far),
        ("list_near_pairs", "list_far_pairs")[far],
        shape(PLAN_LEN, dtype=jnp.int32),
        [pl.BlockSpec(memory_space=pltpu.HBM)],
        SMEM,
        [pltpu.SMEM((BLOCKS, BLOCKS), jnp.int32), pltpu.SemaphoreType.DMA],
        limit=1 << 20,
    )(pltpu.with_memory_space_constraint(owner_table, pltpu.HBM))


def near_call(plan, half):
    return call(
        near_kernel,
        "near_sums",
        [BLOCK_SET, WIDE_SET, shape(*ACC, dtype=F32)],
        [VMEM] * 2,
        [VMEM] * 3,
        PLAN,
    )(plan, half)


def far_call(near_plan, plan, other, near_rows, near_wide, near_acc):
    return call(
        far_kernel,
        "far_sums",
        [BLOCK_SET, WIDE_SET, shape(SENT, ROWS, dtype=F32)],
        [VMEM] * 6,
        [VMEM] * 3,
        [pltpu.VMEM(ACC, F32), pltpu.VMEM((2, SIDE, ROWS), F32), *PLAN, *PLAN],
    )(near_plan, plan, other, near_rows, near_wide, near_acc)


def near_grad_call(plan, near_rows, near_wide, near_sent):
    return call(
        near_grad_kernel,
        "near_gradient",
        [shape(*GRAD, dtype=F32), shape(*COL, dtype=F32)],
        [VMEM] * 4,
        [VMEM] * 2,
        [INV, *PLAN],
    )(plan, near_rows, near_wide, near_sent)


def far_grad_call(*arrays):
    return call(
        far_grad_kernel,
        "far_gradient",
        [shape(HALF + 16, ROWS)] * LINE,
        [VMEM] * 8,
        [VMEM] * LINE,
        [INV, pltpu.VMEM(GRAD, F32), pltpu.VMEM(COL, F32), *PLAN],
    )(*arrays)


def per_device(teacher_q, student_q, owner_table):
    slices = call(
        slice_kernel,
        "slice_heads",
        [shape(ROWS, ROWS)] * LINE,
        [pl.BlockSpec(memory_space=pltpu.HBM)] * 2,
        [VMEM] * LINE,
        [pltpu.VMEM(teacher_q.shape, jnp.bfloat16)] * 2 + [pltpu.SemaphoreType.DMA((2,))],
        limit=2 << 20,
    )(*[pltpu.with_memory_space_constraint(a, pltpu.HBM) for a in (teacher_q, student_q)])
    near_plan, far_plan = plan_call(owner_table, 0), plan_call(owner_table, 1)
    line = jnp.stack([slices[0]] + [exchanged(slices[b], MET_X[b], 3) for b in (1, 2, 3)])
    line, near_plan = lax.optimization_barrier((line, near_plan))
    half = jnp.concatenate([line] + [exchanged(line, MET_Y[a], 1) for a in (1, 2, 3)])
    half, far_plan = lax.optimization_barrier((half, far_plan))
    other = swapped(half)
    near_rows, near_wide, near_acc = near_call(near_plan, half)
    far_rows, far_wide, near_sent = far_call(
        near_plan, far_plan, other, near_rows, near_wide, near_acc
    )
    far_sent = swapped(near_sent)
    near_grad, near_col = near_grad_call(near_plan, near_rows, near_wide, near_sent)
    grads = far_grad_call(
        far_plan, near_rows, far_rows, far_wide, near_sent, far_sent, near_grad, near_col
    )
    back = [grads[0]] + [exchanged(grads[b], MET_BACK[b], 3) for b in (1, 2, 3)]
    return call(
        assemble_kernel,
        "assemble",
        [shape(*teacher_q.shape), shape(LINE, dtype=F32)],
        [VMEM] * LINE,
        [VMEM, SMEM],
        limit=2 << 20,
    )(*back)


def solution(mesh):
    placed = (P("tok", "head"), P("tok", "head"), P())
    return jax.shard_map(
        lambda *arrays: tuple(per_device(*arrays)),
        mesh=mesh,
        in_specs=placed,
        out_specs=(P("tok", "head"), P("head")),
        check_vma=False,
    )
```
